256 devices in a mesh: space: 8 (over y, core), chaos: 32 (over z, x).
Axes of the slice: x: 4, y: 4, z: 8, core: 2. Of those that a mesh axis runs over, the one named last changes fastest.
Arguments:
- source_term: float32 [480, 8, 64, 128], P('chaos', 'space'), may hold values from -17 to 17, as said below
- start_field: float32 [480, 8, 64, 128], P('chaos', 'space'), may hold values from -1.5 to 1.5
- conductivity: float32 [9, 8, 64, 128], P(None, 'space'), may hold values from -0.05 to 3, as said below
- pair_modes: int32 [8, 480, 2], replicated, may hold values from 0 to 479, as said below
- pair_weight: float32 [8, 480], replicated, may hold values from -1 to 1
Outputs:
- solution: float32 [480, 8, 64, 128], P('chaos', 'space')
- residual: float32 [480, 8, 64, 128], P('chaos', 'space')
- direction: float32 [480, 8, 64, 128], P('chaos', 'space')
The draws below stay inside these ranges and needn't reach their ends.
Inputs may be any that keep to these rules, and one draw needn't show every extreme that they name: `source_term`: mode scales differ from mode to mode. conductivity[0] lies in 1 to 3 and every other coefficient field in -0.05 to 0.05. `pair_modes`: for each term, every mode appears in exactly two of the 480 pairs, and no pair joins a mode with itself.
All inputs are finite; a program needn't handle non-finite values.
Results may differ from the reference program's by a relative error of at most 0.0003.
Values sent between devices are 32-bit elements; how exact they have to be, the bound alone decides.
A program may use at most 320 MiB of HBM per device.

```python
import jax
import jax.numpy as jnp

MODES = 480
COUPLED = 8
NY = 64
NZ = 128
PAIRS = 480
NX = 8


def draw_source_term(key, part):
    noise_key, scale_key = jax.random.split(key, 2)
    noise = jnp.clip(jax.random.normal(noise_key, (MODES, NX, NY, NZ), jnp.float32), -6.0, 6.0)
    mode_scale = 2.0 ** (jnp.arange(MODES, dtype=jnp.float32) / MODES)
    mode_scale = mode_scale * jax.random.uniform(scale_key, (MODES,), jnp.float32, 0.7, 1.4)
    return noise * mode_scale[:, None, None, None]


def draw_conductivity(key, part):
    mean_key, other_key = jax.random.split(key, 2)
    mean_field = jax.random.uniform(mean_key, (1, NX, NY, NZ), jnp.float32, 1.0, 3.0)
    others = jax.random.uniform(other_key, (COUPLED, NX, NY, NZ), jnp.float32, -0.05, 0.05)
    return jnp.concatenate([mean_field, others], axis=0)


def draw_pair_modes(key, part):
    keys = jax.random.split(jax.random.fold_in(key, 17), 2 * COUPLED)
    orders = jax.vmap(lambda single: jax.random.permutation(single, MODES))(keys)
    return orders.reshape(COUPLED, 2 * (MODES // 2), 2).astype(jnp.int32)


def levels(key, shape, shards, low, high):
    def one(dim, parts):
        steps = jax.random.uniform(jax.random.fold_in(jax.random.fold_in(key, 6), dim), (parts,), jnp.float32, low / len(shards), high / len(shards))
        return jnp.repeat(jnp.exp(steps), shape[dim] // parts).reshape((-1,) + (1,) * (len(shape) - dim - 1))

    loudness = one(*shards[0])
    for cut in shards[1:]:
        loudness = loudness * one(*cut)
    return loudness


def gaussian(rng, shape, scale, bound, shards=(), kind=jnp.bfloat16):
    values = jax.random.normal(rng, shape, jnp.float32) * scale
    if len(shards) > 0:
        values = levels(rng, shape, shards, -0.22, 0.18) * values
    return jnp.clip(values, min=-bound, max=bound).astype(kind)


def setup_inputs(seed: int = 0) -> dict:
    key_list = jax.random.split(jax.random.key(seed), 6)
    return {
        "source_term": draw_source_term(jax.random.fold_in(key_list[5], 71), 0),
        "start_field": gaussian(key_list[1], (MODES, NX, NY, NZ), 0.1, 1.5, ((0, 32), (1, 8)), jnp.float32),
        "conductivity": draw_conductivity(jax.random.fold_in(key_list[5], 71), 0),
        "pair_modes": draw_pair_modes(jax.random.fold_in(key_list[5], 71), 0),
        "pair_weight": jnp.clip(jax.random.uniform(key_list[4], (COUPLED, PAIRS), jnp.float32, -1.0, 1.0), -1.0, 1.0),
    }


CENTER_BOUND = 1.05
HALF_WIDTH = 0.95
FIRST_COEF = 4.0 * CENTER_BOUND / (2.0 * CENTER_BOUND * CENTER_BOUND - HALF_WIDTH * HALF_WIDTH)
SECOND_COEF = 2.0 / (2.0 * CENTER_BOUND * CENTER_BOUND - HALF_WIDTH * HALF_WIDTH)
NEIGHBOURS = ((1, 0, 0), (-1, 0, 0), (0, 1, 0), (0, -1, 0), (0, 0, 1), (0, 0, -1))
CENTER_OFFSET = (0, 0, 0)


def window(source, offset):
    extent = source.shape
    return source[..., 1 + offset[0]:extent[-3] - 1 + offset[0], 1 + offset[1]:extent[-2] - 1 + offset[1], 1 + offset[2]:extent[-1] - 1 + offset[2]]


def stencil(coef_pad, field_pad):
    center_coef = window(coef_pad, CENTER_OFFSET)
    center_field = window(field_pad, CENTER_OFFSET)
    result = jnp.zeros_like(center_field)
    for offset in NEIGHBOURS:
        result = result + 0.5 * (center_coef + window(coef_pad, offset)) * (center_field - window(field_pad, offset))
    return result


def diagonal_of(coef_pad):
    center_coef = window(coef_pad, CENTER_OFFSET)
    result = jnp.zeros_like(center_coef)
    for offset in NEIGHBOURS:
        result = result + 0.5 * (center_coef + window(coef_pad, offset))
    return result


def couple_modes(values, pair_list, weights):
    mode_count = values.shape[0]
    flattened = values.reshape(mode_count, -1)
    first_mode = pair_list[:, 0].astype(jnp.int32)
    second_mode = pair_list[:, 1].astype(jnp.int32)
    scaled = weights[:, None]
    mixed = jax.ops.segment_sum(scaled * flattened[second_mode], first_mode, num_segments=mode_count)
    mixed = mixed + jax.ops.segment_sum(scaled * flattened[first_mode], second_mode, num_segments=mode_count)
    return mixed.reshape(values.shape)


def pad_grid(values):
    return jnp.pad(values, ((0, 0), (1, 1), (1, 1), (1, 1)))


def reference(source_term, start_field, conductivity, pair_modes, pair_weight):
    coef_pad = pad_grid(conductivity)
    mean_pad = coef_pad[0]
    diagonal = diagonal_of(mean_pad)

    def operate(values):
        summed = stencil(mean_pad, pad_grid(values))
        for term_index in range(COUPLED):
            mixed = couple_modes(values, pair_modes[term_index], pair_weight[term_index])
            summed = summed + stencil(coef_pad[term_index + 1], pad_grid(mixed))
        return summed

    def precondition(values):
        scaled = values / diagonal
        return FIRST_COEF * scaled - SECOND_COEF * stencil(mean_pad, pad_grid(scaled)) / diagonal

    start_residual = source_term - operate(start_field)
    search = precondition(start_residual)
    energy_start = jnp.sum(start_residual * search)
    image_field = operate(search)
    curvature = jnp.sum(search * image_field)
    step_size = energy_start / curvature
    solution = start_field + step_size * search
    residual = start_residual - step_size * image_field
    new_search = precondition(residual)
    energy_next = jnp.sum(residual * new_search)
    direction = new_search + (energy_next / energy_start) * search
    return solution, residual, direction
```

```python
import functools

import jax
import jax.numpy as jnp
from jax import lax
from jax.experimental import pallas as pl
from jax.experimental.pallas import tpu as pltpu
from jax.sharding import PartitionSpec as P

CENTER_BOUND = 1.05
HALF_WIDTH = 0.95
FIRST_COEF = 4.0 * CENTER_BOUND / (2.0 * CENTER_BOUND * CENTER_BOUND - HALF_WIDTH * HALF_WIDTH)
SECOND_COEF = 2.0 / (2.0 * CENTER_BOUND * CENTER_BOUND - HALF_WIDTH * HALF_WIDTH)
SLOT = 16
F32 = jnp.float32
BF16 = jnp.bfloat16
MESH = pl.DeviceIdType.MESH


def al(value, unit):
    return pl.multiple_of(value, unit)


def kernel(
    chaos_n, space_n, terms, own_modes, rows,
    v_ref, f_ref, cond_ref, lists_ref,
    sol_ref, res_ref, dir_ref,
    x0, x1, ft, q_ref, mq_ref, cy, cxm, cxp, c0m, c0p, oc, ob, kf, kb,
    gh, gl, oa, wh, wl, ph, plo, acc,
    t0, t1, hxm0, hxm1, hxp0, hxp1, hym0, hym1, hyp0, hyp1,
    y0, y1, o0, o1, z0, z1, zxm0, zxm1, zxp0, zxp1,
    dots, dsum, dga, dgb,
    coef_sem, send_sem, a2a_sem, fwd_sem, ret_sem, zx_sem, dota_sem, dotb_sem,
):
    me = lax.axis_index("chaos")
    sp = lax.axis_index("space")
    up = lax.rem(sp + 1, space_n)
    down = lax.rem(sp + space_n - 1, space_n)
    right = lax.rem(me + 1, chaos_n)
    left = lax.rem(me + chaos_n - 1, chaos_n)
    slots = chaos_n * SLOT
    flat = rows * SLOT
    width = v_ref.shape[-1]

    def peer(k):
        return lax.rem(me + k, chaos_n)

    def source(k):
        return lax.rem(me + chaos_n - k, chaos_n)

    def block(c):
        return pl.ds(al(c * 32, 32), 32)

    def remote(src, dst, ssem, rsem, target):
        return pltpu.make_async_remote_copy(
            src_ref=src, dst_ref=dst, send_sem=ssem, recv_sem=rsem,
            device_id=target, device_id_type=MESH,
        )

    def drain(ref, count, sem):
        pltpu.make_async_copy(ref.at[pl.ds(0, count)], ref.at[pl.ds(0, count)], sem).wait()

    barrier = pltpu.get_barrier_semaphore()

    def greet_chaos(k, carry):
        pl.semaphore_signal(barrier, inc=1, device_id={"chaos": peer(k)}, device_id_type=MESH)
        return carry

    lax.fori_loop(1, chaos_n, greet_chaos, 0)

    def greet_space(k, carry):
        pl.semaphore_signal(
            barrier, inc=1, device_id={"space": lax.rem(sp + k, space_n)}, device_id_type=MESH
        )
        return carry

    lax.fori_loop(1, space_n, greet_space, 0)

    tiles = rows // 8
    x0[...] = jnp.zeros_like(x0)
    ft[...] = jnp.zeros_like(ft)
    cy[...] = jnp.zeros_like(cy)

    def turn_in(m, carry):
        for tile in range(tiles):
            where = pl.ds(tile * 128 + m, 8, stride=SLOT)
            x0[where, :] = v_ref[m, pl.ds(tile * 8, 8), :]
            ft[where, :] = f_ref[m, pl.ds(tile * 8, 8), :]
        return carry

    lax.fori_loop(0, own_modes, turn_in, 0)
    for j in range(terms + 1):
        for tile in range(tiles):
            cy[pl.ds(tile * 128 + j, 8, stride=SLOT), :] = cond_ref[j, pl.ds(tile * 8, 8), :]

    pl.semaphore_wait(barrier, chaos_n - 1 + space_n - 1)

    coef_copies = (
        remote(cy.at[block(me)], cxm.at[pl.ds(0, 32)], send_sem.at[0], coef_sem.at[0], {"space": up}),
        remote(cy.at[block(me)], cxp.at[pl.ds(0, 32)], send_sem.at[1], coef_sem.at[1], {"space": down}),
        remote(cond_ref.at[0], c0m, send_sem.at[2], coef_sem.at[2], {"space": up}),
        remote(cond_ref.at[0], c0p, send_sem.at[3], coef_sem.at[3], {"space": down}),
    )
    for copy in coef_copies:
        copy.start()

    def send_block(src, dst, ssem, rsems, k):
        c = peer(k)
        remote(src.at[block(c)], dst.at[block(me)], ssem, rsems.at[k], {"chaos": c}).start()

    def send_all(src, dst, ssem, rsems):
        def body(k, carry):
            send_block(src, dst, ssem, rsems, k)
            return carry

        lax.fori_loop(1, chaos_n, body, 0)
        dst[block(me), :] = src[block(me), :]

    send_all(x0, t0, send_sem.at[4], a2a_sem.at[0])

    lane = lax.broadcasted_iota(jnp.int32, (1, width), 1)
    zm_mask = jnp.where(lane > 0, 0.5, 0.0).astype(F32)
    zp_mask = jnp.where(lane < width - 1, 0.5, 0.0).astype(F32)
    xm_mask = jnp.where(sp > 0, 0.5, 0.0).astype(F32)
    xp_mask = jnp.where(sp < space_n - 1, 0.5, 0.0).astype(F32)

    for copy in coef_copies:
        copy.wait()

    for r in range(2):
        y = me * 2 + r
        cn = cy[pl.ds(al(y * SLOT, SLOT), SLOT), :]
        cm = cy[pl.ds(al(lax.rem(y + rows - 1, rows) * SLOT, SLOT), SLOT), :]
        cp = cy[pl.ds(al(lax.rem(y + 1, rows) * SLOT, SLOT), SLOT), :]
        ym_mask = jnp.where(y > 0, 0.5, 0.0).astype(F32)
        yp_mask = jnp.where(y < rows - 1, 0.5, 0.0).astype(F32)
        total = 3.0 * cn
        around = (
            (cxm[pl.ds(r * SLOT, SLOT), :], xm_mask),
            (cxp[pl.ds(r * SLOT, SLOT), :], xp_mask),
            (cm, ym_mask),
            (cp, yp_mask),
            (pltpu.roll(cn, 1, 1), zm_mask),
            (pltpu.roll(cn, width - 1, 1), zp_mask),
        )
        for n, (other, mask) in enumerate(around):
            total = total + other * mask
            kf[pl.ds((r * 7 + n + 1) * SLOT, SLOT), :] = (cn + other) * mask
        kf[pl.ds(r * 7 * SLOT, SLOT), :] = total
    for r in range(2):
        for j in range(terms + 1):
            for n in range(7):
                row = kf[pl.ds((r * 7 + n) * SLOT + j, 1), :]
                kb[pl.ds(((r * (terms + 1) + j) * 7 + n) * 8, 8), :] = jnp.broadcast_to(row, (8, width))

    c0 = cond_ref[0]
    yrow = lax.broadcasted_iota(jnp.int32, (rows, 1), 0)
    around = (
        (c0m[...], xm_mask),
        (c0p[...], xp_mask),
        (pltpu.roll(c0, 1, 0), jnp.where(yrow > 0, 0.5, 0.0).astype(F32)),
        (pltpu.roll(c0, rows - 1, 0), jnp.where(yrow < rows - 1, 0.5, 0.0).astype(F32)),
        (pltpu.roll(c0, 1, 1), zm_mask),
        (pltpu.roll(c0, width - 1, 1), zp_mask),
    )
    diagonal = 3.0 * c0
    for other, mask in around:
        diagonal = diagonal + other * mask
    inverse = 1.0 / diagonal
    oc[6] = inverse
    for n, (other, mask) in enumerate(around):
        oc[n] = SECOND_COEF * ((c0 + other) * mask) * inverse

    def spread(tile, carry):
        for n in range(7):
            group = oc[n, pl.ds(al(tile * 8, 8), 8), :]
            for i in range(8):
                at = al((tile * 56 + i * 7 + n) * 8, 8)
                ob[pl.ds(at, 8), :] = jnp.broadcast_to(group[i : i + 1, :], (8, width))
        return carry

    lax.fori_loop(0, tiles, spread, 0)

    ts, hxms, hxps, hyms, hyps = ((t0, t1), (hxm0, hxm1), (hxp0, hxp1), (hym0, hym1), (hyp0, hyp1))
    ys, os, zs, zxms, zxps = ((y0, y1), (o0, o1), (z0, z1), (zxm0, zxm1), (zxp0, zxp1))

    def forward_block(it, k):
        c = source(k)
        t = ts[it]
        half = pl.ds(al(c * SLOT, SLOT), SLOT)
        rsem = fwd_sem.at[it].at[k]
        base = 8 + it * 8
        remote(t.at[block(c)], hxms[it].at[block(c)], send_sem.at[base], rsem, {"space": up}).start()
        remote(t.at[block(c)], hxps[it].at[block(c)], send_sem.at[base + 1], rsem, {"space": down}).start()
        low = t.at[pl.ds(al(c * 32, 32), SLOT)]
        high = t.at[pl.ds(al(c * 32 + SLOT, SLOT), SLOT)]
        kr = lax.rem(k + 1, chaos_n)
        kl = lax.rem(k + chaos_n - 1, chaos_n)
        remote(high, hyms[it].at[half], send_sem.at[base + 2], fwd_sem.at[it].at[kr], {"chaos": right}).start()
        remote(low, hyps[it].at[half], send_sem.at[base + 3], fwd_sem.at[it].at[kl], {"chaos": left}).start()

    def receive_forward(it, k):
        @pl.when(k > 0)
        def _():
            c = source(k)
            remote(
                ts[it].at[block(c)], ts[it].at[block(c)], send_sem.at[4], a2a_sem.at[it].at[k], {"chaos": left}
            ).wait_recv()

        forward_block(it, k)

    index = lax.broadcasted_iota(jnp.int32, (slots, lists_ref.shape[-1]), 0).astype(F32)
    nt = (((1,), (1,)), ((), ()))
    per = chaos_n // terms if chaos_n >= terms else 1

    def build(j, carry):
        first = lists_ref[pl.ds(j, 1), :]
        second = lists_ref[pl.ds(j + terms, 1), :]
        weight = lists_ref[pl.ds(j + 2 * terms, 1), :]
        weight_high = weight.astype(BF16).astype(F32)
        weight_low = weight - weight_high
        oa[...] = jnp.where(index == first, 1.0, 0.0).astype(BF16)
        here = index == second
        wh[...] = jnp.where(here, weight_high, 0.0).astype(BF16)
        wl[...] = jnp.where(here, weight_low, 0.0).astype(BF16)
        a, b, c = (oa[...], wh[...], wl[...])
        g = lax.dot_general(a, b, nt, preferred_element_type=F32)
        g = g + lax.dot_general(a, c, nt, preferred_element_type=F32)
        g = g + lax.dot_general(b, a, nt, preferred_element_type=F32)
        g = g + lax.dot_general(c, a, nt, preferred_element_type=F32)
        high = g.astype(BF16)
        gh[j] = high
        gl[j] = (g - high.astype(F32)).astype(BF16)

        if chaos_n >= terms:
            for n in range(per):
                receive_forward(0, j * per + n)
        return carry

    lax.fori_loop(0, terms, build, 0)
    if chaos_n < terms:
        for k in range(chaos_n):
            receive_forward(0, jnp.int32(k))

    def operate(it):
        t, hxm, hxp, hym, hyp, y, o = (ts[it], hxms[it], hxps[it], hyms[it], hyps[it], ys[it], os[it])

        def products(k, carry):
            c = source(k)
            drain_ref = hxm.at[pl.ds(0, 96)] if flat >= 96 else None
            pltpu.make_async_copy(drain_ref, drain_ref, fwd_sem.at[it].at[k]).wait()
            for r in range(2):
                for h in range(2):
                    at = pl.ds(al(c * 32 + r * SLOT + h * 8, 8), 8)
                    lo_at = pl.ds(al(c * 32 + h * 8, 8), 8)
                    hi_at = pl.ds(al(c * 32 + SLOT + h * 8, 8), 8)
                    half = pl.ds(al(c * SLOT + h * 8, 8), 8)
                    v = t[at, :]
                    near = (
                        v,
                        hxm[at, :],
                        hxp[at, :],
                        hym[half, :] if r == 0 else t[lo_at, :],
                        t[hi_at, :] if r == 0 else hyp[half, :],
                        pltpu.roll(v, 1, 1),
                        pltpu.roll(v, width - 1, 1),
                    )
                    for j in range(terms + 1):
                        base = (r * (terms + 1) + j) * 56
                        value = kb[pl.ds(base, 8), :] * near[0]
                        for n in range(1, 7):
                            value = value - kb[pl.ds(base + n * 8, 8), :] * near[n]
                        if j == 0:
                            y[at, :] = value
                        else:
                            acc[j - 1, pl.ds(h * 8, 8), :] = value
                for j in range(terms):
                    value = acc[j, pl.ds(0, SLOT), :]
                    high = value.astype(BF16)
                    to = pl.ds(al(c * SLOT, SLOT), SLOT)
                    ph[j, to, pl.ds(r * width, width)] = high
                    plo[j, to, pl.ds(r * width, width)] = (value - high.astype(F32)).astype(BF16)
            return carry

        lax.fori_loop(0, chaos_n, products, 0)

        step = min(slots, 256)
        for part in range(slots // step):
            lines = pl.ds(part * step, step)

            def mix(j, total):
                a, b = (gh[j, lines, :], ph[j])
                total = total + jnp.dot(a, b, preferred_element_type=F32)
                total = total + jnp.dot(a, plo[j], preferred_element_type=F32)
                return total + jnp.dot(gl[j, lines, :], b, preferred_element_type=F32)

            total = lax.fori_loop(0, terms, mix, jnp.zeros((step, 2 * width), F32))
            for c in range(step // SLOT):
                for r in range(2):
                    at = pl.ds(part * step * 2 + c * 32 + r * SLOT, SLOT)
                    y[at, :] = y[at, :] + total[c * SLOT : (c + 1) * SLOT, r * width : (r + 1) * width]
        send_all(y, o, send_sem.at[5 + it], ret_sem.at[it])

    def scaled_rows(it, k, carry):
        c = source(k)
        o, z = (os[it], zs[it])

        @pl.when(k > 0)
        def _():
            remote(o.at[block(c)], o.at[block(c)], send_sem.at[5], ret_sem.at[it].at[k], {"chaos": left}).wait_recv()

        for r in range(2):
            inv = ob[pl.ds(al((c * 2 + r) * 56 + 48, 8), 8), :]
            for h in range(2):
                at = pl.ds(al(c * 32 + r * SLOT + h * 8, 8), 8)
                value = o[at, :]
                if it == 0:
                    value = ft[at, :] - value
                    ft[at, :] = value
                else:
                    q_ref[at, :] = value
                z[at, :] = value * inv
        base = 12 + it * 8
        remote(z.at[block(c)], zxms[it].at[block(c)], send_sem.at[base], zx_sem.at[it].at[k], {"space": up}).start()
        remote(z.at[block(c)], zxps[it].at[block(c)], send_sem.at[base + 1], zx_sem.at[it].at[k], {"space": down}).start()
        return carry

    def precondition(it):
        z, zxm, zxp = (zs[it], zxms[it], zxps[it])
        lax.fori_loop(0, chaos_n, functools.partial(scaled_rows, it), 0)
        zero = jnp.zeros((8, width), F32)

        def finish(k, carry):
            c = source(k)
            sums = carry
            pltpu.make_async_copy(zxm.at[pl.ds(0, 64)], zxm.at[pl.ds(0, 64)], zx_sem.at[it].at[k]).wait()
            for r in range(2):
                line = c * 2 + r
                prev = lax.rem(line + rows - 1, rows)
                after = lax.rem(line + 1, rows)
                coef = [ob[pl.ds(al(line * 56 + n * 8, 8), 8), :] for n in range(6)]
                for h in range(2):
                    at = pl.ds(al(line * SLOT + h * 8, 8), 8)
                    v = z[at, :]
                    near = (
                        zxm[at, :],
                        zxp[at, :],
                        z[pl.ds(al(prev * SLOT + h * 8, 8), 8), :],
                        z[pl.ds(al(after * SLOT + h * 8, 8), 8), :],
                        pltpu.roll(v, 1, 1),
                        pltpu.roll(v, width - 1, 1),
                    )
                    value = (FIRST_COEF - SECOND_COEF) * v
                    for n in range(6):
                        value = value + coef[n] * near[n]
                    if it == 0:
                        x1[at, :] = value
                        sums = (sums[0] + ft[at, :] * value, sums[1])
                    else:
                        mq_ref[at, :] = value
                        image = q_ref[at, :]
                        sums = (sums[0] + x1[at, :] * image, sums[1] + image * value)
            if it == 0:
                @pl.when(k > 0)
                def _():
                    back = lax.rem(chaos_n - k, chaos_n)
                    remote(
                        x1.at[block(c)], t1.at[block(me)], send_sem.at[7], a2a_sem.at[1].at[back], {"chaos": c}
                    ).start()
            return sums

        return lax.fori_loop(0, chaos_n, finish, (zero, zero))

    operate(0)
    energy, _ = precondition(0)
    t1[block(me), :] = x1[block(me), :]

    def take(k, carry):
        receive_forward(1, k)
        return carry

    lax.fori_loop(0, chaos_n, take, 0)
    operate(1)
    curve, image = precondition(1)

    dots[...] = jnp.zeros_like(dots)
    for n, value in enumerate((energy, curve, image)):
        dots[pl.ds(n, 1), :] = jnp.sum(value, axis=0, keepdims=True)

    def tell(k, carry):
        remote(dots, dga.at[k], send_sem.at[24], dota_sem.at[k], {"chaos": peer(k)}).start()
        return carry

    lax.fori_loop(1, chaos_n, tell, 0)

    def hear(k, total):
        remote(dots, dga.at[k], send_sem.at[24], dota_sem.at[k], {"chaos": left}).wait_recv()
        return total + dga[k]

    dsum[...] = lax.fori_loop(1, chaos_n, hear, dots[...])

    def tell_space(k, carry):
        there = lax.rem(sp + k, space_n)
        remote(dsum, dgb.at[k], send_sem.at[25], dotb_sem.at[k], {"space": there}).start()
        return carry

    lax.fori_loop(1, space_n, tell_space, 0)

    def hear_space(k, total):
        remote(dsum, dgb.at[k], send_sem.at[25], dotb_sem.at[k], {"space": up}).wait_recv()
        return total + dgb[k]

    sums = lax.fori_loop(1, space_n, hear_space, dsum[...])
    lanes = jnp.sum(sums, axis=1, keepdims=True)
    energy_start, curvature, image_energy = (lanes[0:1, :], lanes[1:2, :], lanes[2:3, :])
    step_size = energy_start / curvature
    energy_next = energy_start - 2.0 * step_size * curvature + step_size * step_size * image_energy
    ratio = 1.0 + energy_next / energy_start
    step_all = jnp.broadcast_to(step_size, (8, width))
    ratio_all = jnp.broadcast_to(ratio, (8, width))

    def turn_out(m, carry):
        for tile in range(tiles):
            where = pl.ds(tile * 128 + m, 8, stride=SLOT)
            there = pl.ds(tile * 8, 8)
            search = x1[where, :]
            sol_ref[m, there, :] = v_ref[m, there, :] + step_all * search
            res_ref[m, there, :] = ft[where, :] - step_all * q_ref[where, :]
            dir_ref[m, there, :] = ratio_all * search - step_all * mq_ref[where, :]
        return carry

    lax.fori_loop(0, own_modes, turn_out, 0)

    others = chaos_n - 1
    drain(x0, others * 32, send_sem.at[4])
    drain(x1, others * 32, send_sem.at[7])
    for it in range(2):
        drain(ys[it], others * 32, send_sem.at[5 + it])
        for n in range(2):
            drain(ts[it], flat, send_sem.at[8 + it * 8 + n])
            drain(ts[it], flat // 2, send_sem.at[10 + it * 8 + n])
            drain(zs[it], flat, send_sem.at[12 + it * 8 + n])
    pltpu.make_async_copy(dga.at[pl.ds(1, chaos_n - 1)], dga.at[pl.ds(1, chaos_n - 1)], send_sem.at[24]).wait()
    pltpu.make_async_copy(dgb.at[pl.ds(1, space_n - 1)], dgb.at[pl.ds(1, space_n - 1)], send_sem.at[25]).wait()


def per_device(chaos_n, space_n, source_term, start_field, conductivity, pair_modes, pair_weight):
    own_modes, _, rows, width = source_term.shape
    terms, pairs = pair_weight.shape
    slots = chaos_n * SLOT
    flat = rows * SLOT
    padded = -(-pairs // 128) * 128
    ends = pair_modes + pair_modes // own_modes * (SLOT - own_modes)
    lists = jnp.concatenate(
        [ends[:, :, 0].astype(F32), ends[:, :, 1].astype(F32), pair_weight], axis=0
    )
    lists = jnp.pad(lists, ((0, 0), (0, padded - pairs)), constant_values=-1.0)
    field = pltpu.VMEM((flat, width), F32)
    half = pltpu.VMEM((flat // 2, width), F32)
    vmem = pl.BlockSpec(memory_space=pltpu.VMEM)
    shape = jax.ShapeDtypeStruct((own_modes, rows, width), F32)
    outs = pl.pallas_call(
        functools.partial(kernel, chaos_n, space_n, terms, own_modes, rows),
        out_shape=(shape, shape, shape),
        in_specs=[vmem] * 4,
        out_specs=(vmem, vmem, vmem),
        scratch_shapes=[field] * 6
        + [pltpu.VMEM((32, width), F32)] * 2
        + [pltpu.VMEM((rows, width), F32)] * 2
        + [
            pltpu.VMEM((7, rows, width), F32),
            pltpu.VMEM((rows * 56, width), F32),
            pltpu.VMEM((14 * SLOT, width), F32),
            pltpu.VMEM((2 * (terms + 1) * 56, width), F32),
            pltpu.VMEM((terms, slots, slots), BF16),
            pltpu.VMEM((terms, slots, slots), BF16),
            pltpu.VMEM((slots, padded), BF16),
            pltpu.VMEM((slots, padded), BF16),
            pltpu.VMEM((slots, padded), BF16),
            pltpu.VMEM((terms, slots, 2 * width), BF16),
            pltpu.VMEM((terms, slots, 2 * width), BF16),
            pltpu.VMEM((terms, SLOT, width), F32),
        ]
        + [field] * 6
        + [half] * 4
        + [field] * 10
        + [
            pltpu.VMEM((8, width), F32),
            pltpu.VMEM((8, width), F32),
            pltpu.VMEM((chaos_n, 8, width), F32),
            pltpu.VMEM((space_n, 8, width), F32),
            pltpu.SemaphoreType.DMA((4,)),
            pltpu.SemaphoreType.DMA((26,)),
            pltpu.SemaphoreType.DMA((2, chaos_n)),
            pltpu.SemaphoreType.DMA((2, chaos_n)),
            pltpu.SemaphoreType.DMA((2, chaos_n)),
            pltpu.SemaphoreType.DMA((2, chaos_n)),
            pltpu.SemaphoreType.DMA((chaos_n,)),
            pltpu.SemaphoreType.DMA((space_n,)),
        ],
        compiler_params=pltpu.CompilerParams(
            collective_id=0, has_side_effects=True, vmem_limit_bytes=60 * 1024 * 1024
        ),
    )(
        start_field.reshape(own_modes, rows, width),
        source_term.reshape(own_modes, rows, width),
        conductivity.reshape(terms + 1, rows, width),
        lists,
    )
    return tuple(out.reshape(source_term.shape) for out in outs)


def solution(mesh):
    chaos_n, space_n = (mesh.shape["chaos"], mesh.shape["space"])
    field = P("chaos", "space", None, None)
    return jax.shard_map(
        functools.partial(per_device, chaos_n, space_n),
        mesh=mesh,
        in_specs=(field, field, P(None, "space", None, None), P(), P()),
        out_specs=(field, field, field),
        check_vma=False,
    )
```

```python
import functools

import jax
import jax.numpy as jnp
from jax import lax
from jax.experimental import pallas as pl
from jax.experimental.pallas import tpu as pltpu
from jax.sharding import PartitionSpec as P

CENTER_BOUND = 1.05
HALF_WIDTH = 0.95
FIRST_COEF = 4.0 * CENTER_BOUND / (2.0 * CENTER_BOUND * CENTER_BOUND - HALF_WIDTH * HALF_WIDTH)
SECOND_COEF = 2.0 / (2.0 * CENTER_BOUND * CENTER_BOUND - HALF_WIDTH * HALF_WIDTH)
SLOT = 16
F32 = jnp.float32
BF16 = jnp.bfloat16
MESH = pl.DeviceIdType.MESH


def al(value, unit):
    return pl.multiple_of(value, unit)


def kernel(
    chaos_n, space_n, terms, own_modes, rows,
    v_ref, f_ref, cond_ref, lists_ref,
    sol_ref, res_ref, dir_ref,
    xv, xf, rr, ss, qq, mq, zr, zrm, zrp, zq, zqm, zqp,
    tv, tf, tr, tz, ts, tw, y0, y1,
    vxm, vxp, zxm, zxp, sxm, sxp, wxm, wxp,
    vym, vyp, zym, zyp, sym, syp, wym, wyp,
    cy, cxm, cxp, c0m, c0p, oc, ob, kf, kb, tb,
    gh, gl, oa, wh, wl, ph, plo, acc,
    sums, dots, dsum, dga, dgb,
    coef_sem, send_sem, a2a_sem, halo_sem, slab_sem, dota_sem, dotb_sem,
):
    me = lax.axis_index("chaos")
    sp = lax.axis_index("space")
    up = lax.rem(sp + 1, space_n)
    down = lax.rem(sp + space_n - 1, space_n)
    right = lax.rem(me + 1, chaos_n)
    left = lax.rem(me + chaos_n - 1, chaos_n)
    slots = chaos_n * SLOT
    flat = rows * SLOT
    width = v_ref.shape[-1]
    tiles = rows // 8
    per = -(-chaos_n // (terms // 2))
    lag = max(2, chaos_n // 4)

    def swing(i):
        return (2 * lax.rem(i, 2) - 1) * ((i + 1) // 2)

    def target(i):
        return lax.rem(me + chaos_n + swing(i), chaos_n)

    def source(i):
        return lax.rem(me + chaos_n - swing(i), chaos_n)

    def block(c):
        return pl.ds(al(c * 32, 32), 32)

    def low(c):
        return pl.ds(al(c * 32, 32), SLOT)

    def high(c):
        return pl.ds(al(c * 32 + SLOT, SLOT), SLOT)

    def half(c):
        return pl.ds(al(c * SLOT, SLOT), SLOT)

    def remote(src, dst, ssem, rsem, device):
        return pltpu.make_async_remote_copy(
            src_ref=src, dst_ref=dst, send_sem=ssem, recv_sem=rsem,
            device_id=device, device_id_type=MESH,
        )

    def drain(ref, count, sem):
        pltpu.make_async_copy(ref.at[pl.ds(0, count)], ref.at[pl.ds(0, count)], sem).wait()

    barrier = pltpu.get_barrier_semaphore()

    def greet_chaos(k, carry):
        pl.semaphore_signal(
            barrier, inc=1, device_id={"chaos": lax.rem(me + k, chaos_n)}, device_id_type=MESH
        )
        return carry

    lax.fori_loop(1, chaos_n, greet_chaos, 0)

    def greet_space(k, carry):
        pl.semaphore_signal(
            barrier, inc=1, device_id={"space": lax.rem(sp + k, space_n)}, device_id_type=MESH
        )
        return carry

    lax.fori_loop(1, space_n, greet_space, 0)

    blank = jnp.zeros((8, width), F32)

    def turn_in(from_ref, to_ref):
        def body(m, carry):
            for tile in range(tiles):
                to_ref[pl.ds(tile * 128 + m, 8, stride=SLOT), :] = from_ref[m, pl.ds(tile * 8, 8), :]
            return carry

        lax.fori_loop(0, own_modes, body, 0)
        for m in range(own_modes, SLOT):
            for tile in range(tiles):
                to_ref[pl.ds(tile * 128 + m, 8, stride=SLOT), :] = blank

    turn_in(v_ref, xv)
    for j in range(SLOT):
        for tile in range(tiles):
            value = cond_ref[j, pl.ds(tile * 8, 8), :] if j <= terms else blank
            cy[pl.ds(tile * 128 + j, 8, stride=SLOT), :] = value

    pl.semaphore_wait(barrier, chaos_n - 1 + space_n - 1)

    coef_copies = (
        remote(cy.at[block(me)], cxm.at[pl.ds(0, 32)], send_sem.at[0], coef_sem.at[0], {"space": up}),
        remote(cy.at[block(me)], cxp.at[pl.ds(0, 32)], send_sem.at[1], coef_sem.at[1], {"space": down}),
        remote(cond_ref.at[0], c0m, send_sem.at[2], coef_sem.at[2], {"space": up}),
        remote(cond_ref.at[0], c0p, send_sem.at[3], coef_sem.at[3], {"space": down}),
    )
    for copy in coef_copies:
        copy.start()

    def scatter(src, dst, which):
        def body(i, carry):
            c = target(i)
            remote(
                src.at[block(c)], dst.at[block(me)], send_sem.at[4 + which], a2a_sem.at[which].at[me], {"chaos": c}
            ).start()
            return carry

        lax.fori_loop(1, chaos_n, body, 0)
        dst[block(me), :] = src[block(me), :]

    def arrived(dst, which, i):
        @pl.when(i > 0)
        def _():
            c = source(i)
            remote(
                dst.at[block(c)], dst.at[block(c)], send_sem.at[4], a2a_sem.at[which].at[c], {"chaos": left}
            ).wait_recv()

    def spread_halo(src, halo, which, i):
        c = source(i)
        xm, xp, ym, yp = halo
        rsem = halo_sem.at[which].at[c]
        base = 8 + which * 4
        remote(src.at[block(c)], xm.at[block(c)], send_sem.at[base], rsem, {"space": up}).start()
        remote(src.at[block(c)], xp.at[block(c)], send_sem.at[base + 1], rsem, {"space": down}).start()
        remote(src.at[high(c)], ym.at[half(c)], send_sem.at[base + 2], rsem, {"chaos": right}).start()
        remote(src.at[low(c)], yp.at[half(c)], send_sem.at[base + 3], rsem, {"chaos": left}).start()

    def halo_arrived(which, i):
        c = source(i)
        pltpu.make_async_copy(xv.at[pl.ds(0, 96)], xv.at[pl.ds(0, 96)], halo_sem.at[which].at[c]).wait()

    def around(src, halo, c, r, h):
        xm, xp, ym, yp = halo
        at = pl.ds(al(c * 32 + r * SLOT + h * 8, 8), 8)
        other = pl.ds(al(c * 32 + (1 - r) * SLOT + h * 8, 8), 8)
        side = pl.ds(al(c * SLOT + h * 8, 8), 8)
        v = src[at, :]
        return (
            v,
            xm[at, :],
            xp[at, :],
            ym[side, :] if r == 0 else src[other, :],
            src[other, :] if r == 0 else yp[side, :],
            pltpu.roll(v, 1, 1),
            pltpu.roll(v, width - 1, 1),
        )

    scatter(xv, tv, 0)
    turn_in(f_ref, xf)
    scatter(xf, tf, 1)

    lane = lax.broadcasted_iota(jnp.int32, (1, width), 1)
    zm_mask = jnp.where(lane > 0, 0.5, 0.0).astype(F32)
    zp_mask = jnp.where(lane < width - 1, 0.5, 0.0).astype(F32)
    xm_mask = jnp.where(sp > 0, 0.5, 0.0).astype(F32)
    xp_mask = jnp.where(sp < space_n - 1, 0.5, 0.0).astype(F32)

    for copy in coef_copies:
        copy.wait()

    for r in range(2):
        y = me * 2 + r
        cn = cy[pl.ds(al(y * SLOT, SLOT), SLOT), :]
        cm = cy[pl.ds(al(lax.rem(y + rows - 1, rows) * SLOT, SLOT), SLOT), :]
        cp = cy[pl.ds(al(lax.rem(y + 1, rows) * SLOT, SLOT), SLOT), :]
        ym_mask = jnp.where(y > 0, 0.5, 0.0).astype(F32)
        yp_mask = jnp.where(y < rows - 1, 0.5, 0.0).astype(F32)
        total = 3.0 * cn
        near = (
            (cxm[pl.ds(r * SLOT, SLOT), :], xm_mask),
            (cxp[pl.ds(r * SLOT, SLOT), :], xp_mask),
            (cm, ym_mask),
            (cp, yp_mask),
            (pltpu.roll(cn, 1, 1), zm_mask),
            (pltpu.roll(cn, width - 1, 1), zp_mask),
        )
        for n, (other, mask) in enumerate(near):
            total = total + other * mask
            kf[pl.ds((r * 7 + n + 1) * SLOT, SLOT), :] = (cn + other) * mask
        kf[pl.ds(r * 7 * SLOT, SLOT), :] = total
    for r in range(2):
        for j in range(terms + 1):
            for n in range(7):
                row = kf[pl.ds((r * 7 + n) * SLOT + j, 1), :]
                kb[pl.ds(((r * (terms + 1) + j) * 7 + n) * 8, 8), :] = jnp.broadcast_to(row, (8, width))
        inv = 1.0 / kf[pl.ds(r * 7 * SLOT, 1), :]
        tb[pl.ds(r * 56 + 48, 8), :] = jnp.broadcast_to(inv, (8, width))
        for n in range(6):
            row = SECOND_COEF * kf[pl.ds((r * 7 + n + 1) * SLOT, 1), :] * inv
            tb[pl.ds(r * 56 + n * 8, 8), :] = jnp.broadcast_to(row, (8, width))

    c0 = cond_ref[0]
    yrow = lax.broadcasted_iota(jnp.int32, (rows, 1), 0)
    near = (
        (c0m[...], xm_mask),
        (c0p[...], xp_mask),
        (pltpu.roll(c0, 1, 0), jnp.where(yrow > 0, 0.5, 0.0).astype(F32)),
        (pltpu.roll(c0, rows - 1, 0), jnp.where(yrow < rows - 1, 0.5, 0.0).astype(F32)),
        (pltpu.roll(c0, 1, 1), zm_mask),
        (pltpu.roll(c0, width - 1, 1), zp_mask),
    )
    diagonal = 3.0 * c0
    for other, mask in near:
        diagonal = diagonal + other * mask
    inverse = 1.0 / diagonal
    oc[6] = inverse
    for n, (other, mask) in enumerate(near):
        oc[n] = SECOND_COEF * ((c0 + other) * mask) * inverse

    def spread(tile, carry):
        for n in range(7):
            group = oc[n, pl.ds(al(tile * 8, 8), 8), :]
            for i in range(8):
                at = al((tile * 56 + i * 7 + n) * 8, 8)
                ob[pl.ds(at, 8), :] = jnp.broadcast_to(group[i : i + 1, :], (8, width))
        return carry

    lax.fori_loop(0, tiles, spread, 0)

    def products(src, halo, which, y, i):
        halo_arrived(which, i)
        c = source(i)
        to = half(c)
        for r in range(2):
            for h in range(2):
                near = around(src, halo, c, r, h)
                for j in range(terms + 1):
                    base = (r * (terms + 1) + j) * 56
                    value = kb[pl.ds(base, 8), :] * near[0]
                    for n in range(1, 7):
                        value = value - kb[pl.ds(base + n * 8, 8), :] * near[n]
                    if j == 0:
                        y[pl.ds(al(c * 32 + r * SLOT + h * 8, 8), 8), :] = value
                    else:
                        acc[j - 1, pl.ds(h * 8, 8), :] = value
            for j in range(terms):
                value = acc[j, pl.ds(0, SLOT), :]
                top = value.astype(BF16)
                ph[j, to, pl.ds(r * width, width)] = top
                plo[j, to, pl.ds(r * width, width)] = (value - top.astype(F32)).astype(BF16)

    def mix(y):
        def body(j, total):
            a, b = (gh[j], ph[j])
            total = total + jnp.dot(a, b, preferred_element_type=F32)
            total = total + jnp.dot(a, plo[j], preferred_element_type=F32)
            return total + jnp.dot(gl[j], b, preferred_element_type=F32)

        total = lax.fori_loop(0, terms, body, jnp.zeros((slots, 2 * width), F32))
        for c in range(chaos_n):
            for r in range(2):
                at = pl.ds(c * 32 + r * SLOT, SLOT)
                y[at, :] = y[at, :] + total[c * SLOT : (c + 1) * SLOT, r * width : (r + 1) * width]

    index = lax.broadcasted_iota(jnp.int32, (slots, lists_ref.shape[-1]), 0).astype(F32)
    nt = (((1,), (1,)), ((), ()))

    def build(j, carry):
        first = lists_ref[pl.ds(j, 1), :]
        second = lists_ref[pl.ds(j + terms, 1), :]
        weight = lists_ref[pl.ds(j + 2 * terms, 1), :]
        weight_high = weight.astype(BF16).astype(F32)
        weight_low = weight - weight_high
        oa[...] = jnp.where(index == first, 1.0, 0.0).astype(BF16)
        here = index == second
        wh[...] = jnp.where(here, weight_high, 0.0).astype(BF16)
        wl[...] = jnp.where(here, weight_low, 0.0).astype(BF16)
        a, b, c = (oa[...], wh[...], wl[...])
        g = lax.dot_general(a, b, nt, preferred_element_type=F32)
        g = g + lax.dot_general(a, c, nt, preferred_element_type=F32)
        g = g + lax.dot_general(b, a, nt, preferred_element_type=F32)
        g = g + lax.dot_general(c, a, nt, preferred_element_type=F32)
        top = g.astype(BF16)
        gh[j] = top
        gl[j] = (g - top.astype(F32)).astype(BF16)

        def step(n, inner):
            i = (j - terms // 2) * per + n

            @pl.when(i >= 0)
            def _():
                arrived(tv, 0, i)
                spread_halo(tv, (vxm, vxp, vym, vyp), 0, i)

            @pl.when(i >= lag)
            def _():
                products(tv, (vxm, vxp, vym, vyp), 0, y0, i - lag)

            return inner

        return lax.fori_loop(0, per, step, carry)

    lax.fori_loop(0, terms, build, 0)

    def rest(i, carry):
        products(tv, (vxm, vxp, vym, vyp), 0, y0, i)
        return carry

    lax.fori_loop(chaos_n - lag, chaos_n, rest, 0)
    mix(y0)

    sums[...] = jnp.zeros_like(sums)

    def weigh(row, value):
        sums[pl.ds(row * 8, 8), :] = sums[pl.ds(row * 8, 8), :] + value

    def residual_step(i):
        arrived(tf, 1, i)
        c = source(i)
        for r in range(2):
            inv = tb[pl.ds(r * 56 + 48, 8), :]
            for h in range(2):
                at = pl.ds(al(c * 32 + r * SLOT + h * 8, 8), 8)
                value = tf[at, :] - y0[at, :]
                tr[at, :] = value
                tz[at, :] = value * inv
        spread_halo(tz, (zxm, zxp, zym, zyp), 1, i)

        @pl.when(i > 0)
        def _():
            remote(
                tr.at[block(c)], rr.at[block(me)], send_sem.at[6], a2a_sem.at[2].at[me], {"chaos": c}
            ).start()

    def search_step(i):
        halo_arrived(1, i)
        c = source(i)
        for r in range(2):
            coef = [tb[pl.ds(r * 56 + n * 8, 8), :] for n in range(6)]
            for h in range(2):
                at = pl.ds(al(c * 32 + r * SLOT + h * 8, 8), 8)
                near = around(tz, (zxm, zxp, zym, zyp), c, r, h)
                value = (FIRST_COEF - SECOND_COEF) * near[0]
                for n in range(6):
                    value = value + coef[n] * near[n + 1]
                ts[at, :] = value
                weigh(0, value * tr[at, :])
        spread_halo(ts, (sxm, sxp, sym, syp), 2, i)

    def chain(i, carry):
        @pl.when(i < chaos_n)
        def _():
            residual_step(i)

        @pl.when((i >= lag) & (i < chaos_n + lag))
        def _():
            search_step(i - lag)

        @pl.when(i >= 2 * lag)
        def _():
            products(ts, (sxm, sxp, sym, syp), 2, y1, i - 2 * lag)

        return carry

    lax.fori_loop(0, chaos_n + 2 * lag, chain, 0)
    rr[block(me), :] = tr[block(me), :]
    mix(y1)
    scatter(y1, qq, 3)

    def image_step(i, carry):
        c = source(i)
        for r in range(2):
            inv = tb[pl.ds(r * 56 + 48, 8), :]
            for h in range(2):
                at = pl.ds(al(c * 32 + r * SLOT + h * 8, 8), 8)
                tw[at, :] = y1[at, :] * inv
        spread_halo(tw, (wxm, wxp, wym, wyp), 3, i)
        return carry

    lax.fori_loop(0, chaos_n, image_step, 0)

    def slab_step(src, which, z, zm, zp, base, number):
        def body(i, carry):
            arrived(src, which, i)
            c = source(i)
            for r in range(2):
                inv = ob[pl.ds(al((c * 2 + r) * 56 + 48, 8), 8), :]
                for h in range(2):
                    at = pl.ds(al(c * 32 + r * SLOT + h * 8, 8), 8)
                    z[at, :] = src[at, :] * inv
            rsem = slab_sem.at[number].at[c]
            remote(z.at[block(c)], zm.at[block(c)], send_sem.at[base], rsem, {"space": up}).start()
            remote(z.at[block(c)], zp.at[block(c)], send_sem.at[base + 1], rsem, {"space": down}).start()
            return carry

        lax.fori_loop(0, chaos_n, body, 0)

    def slab_finish(z, zm, zp, number, to):
        def body(i, carry):
            c = source(i)
            pltpu.make_async_copy(xv.at[pl.ds(0, 64)], xv.at[pl.ds(0, 64)], slab_sem.at[number].at[c]).wait()
            for r in range(2):
                line = c * 2 + r
                prev = lax.rem(line + rows - 1, rows)
                after = lax.rem(line + 1, rows)
                coef = [ob[pl.ds(al(line * 56 + n * 8, 8), 8), :] for n in range(6)]
                for h in range(2):
                    at = pl.ds(al(line * SLOT + h * 8, 8), 8)
                    v = z[at, :]
                    near = (
                        zm[at, :],
                        zp[at, :],
                        z[pl.ds(al(prev * SLOT + h * 8, 8), 8), :],
                        z[pl.ds(al(after * SLOT + h * 8, 8), 8), :],
                        pltpu.roll(v, 1, 1),
                        pltpu.roll(v, width - 1, 1),
                    )
                    value = (FIRST_COEF - SECOND_COEF) * v
                    for n in range(6):
                        value = value + coef[n] * near[n]
                    to[at, :] = value
            return carry

        lax.fori_loop(0, chaos_n, body, 0)

    slab_step(rr, 2, zr, zrm, zrp, 24, 0)

    def image_dot(i, carry):
        halo_arrived(3, i)
        c = source(i)
        for r in range(2):
            coef = [tb[pl.ds(r * 56 + n * 8, 8), :] for n in range(6)]
            for h in range(2):
                at = pl.ds(al(c * 32 + r * SLOT + h * 8, 8), 8)
                near = around(tw, (wxm, wxp, wym, wyp), c, r, h)
                value = (FIRST_COEF - SECOND_COEF) * near[0]
                for n in range(6):
                    value = value + coef[n] * near[n + 1]
                image = y1[at, :]
                weigh(1, image * ts[at, :])
                weigh(2, image * value)
        return carry

    lax.fori_loop(0, chaos_n, image_dot, 0)
    dots[...] = blank
    for n in range(3):
        dots[pl.ds(n, 1), :] = jnp.sum(sums[pl.ds(n * 8, 8), :], axis=0, keepdims=True)

    def tell(k, carry):
        c = lax.rem(me + k, chaos_n)
        remote(dots, dga.at[k], send_sem.at[28], dota_sem.at[k], {"chaos": c}).start()
        return carry

    lax.fori_loop(1, chaos_n, tell, 0)

    slab_finish(zr, zrm, zrp, 0, ss)

    def hear(k, total):
        remote(dots, dga.at[k], send_sem.at[28], dota_sem.at[k], {"chaos": left}).wait_recv()
        return total + dga[k]

    dsum[...] = lax.fori_loop(1, chaos_n, hear, dots[...])

    def tell_space(k, carry):
        there = lax.rem(sp + k, space_n)
        remote(dsum, dgb.at[k], send_sem.at[29], dotb_sem.at[k], {"space": there}).start()
        return carry

    lax.fori_loop(1, space_n, tell_space, 0)

    slab_step(qq, 3, zq, zqm, zqp, 26, 1)
    slab_finish(zq, zqm, zqp, 1, mq)

    def hear_space(k, total):
        remote(dsum, dgb.at[k], send_sem.at[29], dotb_sem.at[k], {"space": up}).wait_recv()
        return total + dgb[k]

    whole = lax.fori_loop(1, space_n, hear_space, dsum[...])
    lanes = jnp.sum(whole, axis=1, keepdims=True)
    energy_start, curvature, image_energy = (lanes[0:1, :], lanes[1:2, :], lanes[2:3, :])
    step_size = energy_start / curvature
    energy_next = energy_start - 2.0 * step_size * curvature + step_size * step_size * image_energy
    ratio = 1.0 + energy_next / energy_start
    step_all = jnp.broadcast_to(step_size, (8, width))
    ratio_all = jnp.broadcast_to(ratio, (8, width))

    def turn_out(m, carry):
        for tile in range(tiles):
            where = pl.ds(tile * 128 + m, 8, stride=SLOT)
            there = pl.ds(tile * 8, 8)
            search = ss[where, :]
            sol_ref[m, there, :] = v_ref[m, there, :] + step_all * search
            res_ref[m, there, :] = rr[where, :] - step_all * qq[where, :]
            dir_ref[m, there, :] = ratio_all * search - step_all * mq[where, :]
        return carry

    lax.fori_loop(0, own_modes, turn_out, 0)

    for n, ref in enumerate((xv, xf, tr, y1)):
        drain(ref, (chaos_n - 1) * 32, send_sem.at[4 + n])
    for n, ref in enumerate((tv, tz, ts, tw)):
        for m, count in enumerate((flat, flat, flat // 2, flat // 2)):
            drain(ref, count, send_sem.at[8 + n * 4 + m])
    for n, ref in enumerate((zr, zq)):
        for m in range(2):
            drain(ref, flat, send_sem.at[24 + n * 2 + m])
    pltpu.make_async_copy(dga.at[pl.ds(1, chaos_n - 1)], dga.at[pl.ds(1, chaos_n - 1)], send_sem.at[28]).wait()
    pltpu.make_async_copy(dgb.at[pl.ds(1, space_n - 1)], dgb.at[pl.ds(1, space_n - 1)], send_sem.at[29]).wait()


def per_device(chaos_n, space_n, source_term, start_field, conductivity, pair_modes, pair_weight):
    own_modes, _, rows, width = source_term.shape
    terms, pairs = pair_weight.shape
    slots = chaos_n * SLOT
    flat = rows * SLOT
    padded = -(-pairs // 128) * 128
    ends = pair_modes + pair_modes // own_modes * (SLOT - own_modes)
    lists = jnp.concatenate(
        [ends[:, :, 0].astype(F32), ends[:, :, 1].astype(F32), pair_weight], axis=0
    )
    lists = jnp.pad(lists, ((0, 0), (0, padded - pairs)), constant_values=-1.0)
    field = pltpu.VMEM((flat, width), F32)
    half = pltpu.VMEM((flat // 2, width), F32)
    vmem = pl.BlockSpec(memory_space=pltpu.VMEM)
    shape = jax.ShapeDtypeStruct((own_modes, rows, width), F32)
    outs = pl.pallas_call(
        functools.partial(kernel, chaos_n, space_n, terms, own_modes, rows),
        out_shape=(shape, shape, shape),
        in_specs=[vmem] * 4,
        out_specs=(vmem, vmem, vmem),
        scratch_shapes=[field] * 28
        + [half] * 8
        + [field]
        + [pltpu.VMEM((32, width), F32)] * 2
        + [pltpu.VMEM((rows, width), F32)] * 2
        + [
            pltpu.VMEM((7, rows, width), F32),
            pltpu.VMEM((rows * 56, width), F32),
            pltpu.VMEM((14 * SLOT, width), F32),
            pltpu.VMEM((2 * (terms + 1) * 56, width), F32),
            pltpu.VMEM((112, width), F32),
            pltpu.VMEM((terms, slots, slots), BF16),
            pltpu.VMEM((terms, slots, slots), BF16),
            pltpu.VMEM((slots, padded), BF16),
            pltpu.VMEM((slots, padded), BF16),
            pltpu.VMEM((slots, padded), BF16),
            pltpu.VMEM((terms, slots, 2 * width), BF16),
            pltpu.VMEM((terms, slots, 2 * width), BF16),
            pltpu.VMEM((terms, SLOT, width), F32),
            pltpu.VMEM((24, width), F32),
            pltpu.VMEM((8, width), F32),
            pltpu.VMEM((8, width), F32),
            pltpu.VMEM((chaos_n, 8, width), F32),
            pltpu.VMEM((space_n, 8, width), F32),
            pltpu.SemaphoreType.DMA((4,)),
            pltpu.SemaphoreType.DMA((30,)),
            pltpu.SemaphoreType.DMA((4, chaos_n)),
            pltpu.SemaphoreType.DMA((4, chaos_n)),
            pltpu.SemaphoreType.DMA((2, chaos_n)),
            pltpu.SemaphoreType.DMA((chaos_n,)),
            pltpu.SemaphoreType.DMA((space_n,)),
        ],
        compiler_params=pltpu.CompilerParams(
            collective_id=0, has_side_effects=True, vmem_limit_bytes=60 * 1024 * 1024
        ),
    )(
        start_field.reshape(own_modes, rows, width),
        source_term.reshape(own_modes, rows, width),
        conductivity.reshape(terms + 1, rows, width),
        lists,
    )
    return tuple(out.reshape(source_term.shape) for out in outs)


def solution(mesh):
    chaos_n, space_n = (mesh.shape["chaos"], mesh.shape["space"])
    field = P("chaos", "space", None, None)
    return jax.shard_map(
        functools.partial(per_device, chaos_n, space_n),
        mesh=mesh,
        in_specs=(field, field, P(None, "space", None, None), P(), P()),
        out_specs=(field, field, field),
        check_vma=False,
    )
```

```python
import functools

import jax
import jax.numpy as jnp
from jax import lax
from jax.experimental import pallas as pl
from jax.experimental.pallas import tpu as pltpu
from jax.sharding import PartitionSpec as P

CENTER_BOUND = 1.05
HALF_WIDTH = 0.95
FIRST_COEF = 4.0 * CENTER_BOUND / (2.0 * CENTER_BOUND * CENTER_BOUND - HALF_WIDTH * HALF_WIDTH)
SECOND_COEF = 2.0 / (2.0 * CENTER_BOUND * CENTER_BOUND - HALF_WIDTH * HALF_WIDTH)
SLOT = 16
F32 = jnp.float32
BF16 = jnp.bfloat16
MESH = pl.DeviceIdType.MESH


def al(value, unit):
    return pl.multiple_of(value, unit)


def kernel(
    chaos_n, space_n, terms, own_modes, rows,
    v_ref, f_ref, cond_ref, lists_ref,
    sol_ref, res_ref, dir_ref,
    xv, xf, rr, ss, qq, mq, zr, zrm, zrp, zq, zqm, zqp,
    tv, tf, tr, tz, ts, tw, y0, y1,
    vxm, vxp, zxm, zxp, sxm, sxp, wxm, wxp,
    vym, vyp, zym, zyp, sym, syp, wym, wyp,
    cy, cxm, cxp, c0m, c0p, oc, ob, kf, kb, tb,
    gh, gl, oa, wh, wl, ph, plo, acc,
    sums, dots, dsum, dga, dgb,
    coef_sem, send_sem, a2a_sem, halo_sem, slab_sem, dota_sem, dotb_sem,
):
    me = lax.axis_index("chaos")
    sp = lax.axis_index("space")
    up = lax.rem(sp + 1, space_n)
    down = lax.rem(sp + space_n - 1, space_n)
    right = lax.rem(me + 1, chaos_n)
    left = lax.rem(me + chaos_n - 1, chaos_n)
    slots = chaos_n * SLOT
    flat = rows * SLOT
    width = v_ref.shape[-1]
    tiles = rows // 8
    per = -(-chaos_n // terms)
    lag = max(2, chaos_n // 2)

    def swing(i):
        return (2 * lax.rem(i, 2) - 1) * ((i + 1) // 2)

    def target(i):
        return lax.rem(me + chaos_n + swing(i), chaos_n)

    def source(i):
        return lax.rem(me + chaos_n - swing(i), chaos_n)

    def block(c):
        return pl.ds(al(c * 32, 32), 32)

    def low(c):
        return pl.ds(al(c * 32, 32), SLOT)

    def high(c):
        return pl.ds(al(c * 32 + SLOT, SLOT), SLOT)

    def half(c):
        return pl.ds(al(c * SLOT, SLOT), SLOT)

    def remote(src, dst, ssem, rsem, device):
        return pltpu.make_async_remote_copy(
            src_ref=src, dst_ref=dst, send_sem=ssem, recv_sem=rsem,
            device_id=device, device_id_type=MESH,
        )

    def drain(ref, count, sem):
        pltpu.make_async_copy(ref.at[pl.ds(0, count)], ref.at[pl.ds(0, count)], sem).wait()

    barrier = pltpu.get_barrier_semaphore()

    def greet_chaos(k, carry):
        pl.semaphore_signal(
            barrier, inc=1, device_id={"chaos": lax.rem(me + k, chaos_n)}, device_id_type=MESH
        )
        return carry

    lax.fori_loop(1, chaos_n, greet_chaos, 0)

    def greet_space(k, carry):
        pl.semaphore_signal(
            barrier, inc=1, device_id={"space": lax.rem(sp + k, space_n)}, device_id_type=MESH
        )
        return carry

    lax.fori_loop(1, space_n, greet_space, 0)

    blank = jnp.zeros((8, width), F32)

    def turn_in(from_ref, to_ref):
        def body(m, carry):
            for tile in range(tiles):
                to_ref[pl.ds(tile * 128 + m, 8, stride=SLOT), :] = from_ref[m, pl.ds(tile * 8, 8), :]
            return carry

        lax.fori_loop(0, own_modes, body, 0)
        for m in range(own_modes, SLOT):
            for tile in range(tiles):
                to_ref[pl.ds(tile * 128 + m, 8, stride=SLOT), :] = blank

    turn_in(v_ref, xv)
    for j in range(SLOT):
        for tile in range(tiles):
            value = cond_ref[j, pl.ds(tile * 8, 8), :] if j <= terms else blank
            cy[pl.ds(tile * 128 + j, 8, stride=SLOT), :] = value

    pl.semaphore_wait(barrier, chaos_n - 1 + space_n - 1)

    coef_copies = (
        remote(cy.at[block(me)], cxm.at[pl.ds(0, 32)], send_sem.at[0], coef_sem.at[0], {"space": up}),
        remote(cy.at[block(me)], cxp.at[pl.ds(0, 32)], send_sem.at[1], coef_sem.at[1], {"space": down}),
        remote(cond_ref.at[0], c0m, send_sem.at[2], coef_sem.at[2], {"space": up}),
        remote(cond_ref.at[0], c0p, send_sem.at[3], coef_sem.at[3], {"space": down}),
    )
    for copy in coef_copies:
        copy.start()

    def scatter(src, dst, which):
        def body(i, carry):
            c = target(i)
            remote(
                src.at[block(c)], dst.at[block(me)], send_sem.at[4 + which], a2a_sem.at[which].at[me], {"chaos": c}
            ).start()
            return carry

        lax.fori_loop(1, chaos_n, body, 0)
        dst[block(me), :] = src[block(me), :]

    def arrived(dst, which, i):
        @pl.when(i > 0)
        def _():
            c = source(i)
            remote(
                dst.at[block(c)], dst.at[block(c)], send_sem.at[4], a2a_sem.at[which].at[c], {"chaos": left}
            ).wait_recv()

    def spread_halo(src, halo, which, i):
        c = source(i)
        xm, xp, ym, yp = halo
        rsem = halo_sem.at[which].at[c]
        base = 8 + which * 4
        remote(src.at[block(c)], xm.at[block(c)], send_sem.at[base], rsem, {"space": up}).start()
        remote(src.at[block(c)], xp.at[block(c)], send_sem.at[base + 1], rsem, {"space": down}).start()
        remote(src.at[high(c)], ym.at[half(c)], send_sem.at[base + 2], rsem, {"chaos": right}).start()
        remote(src.at[low(c)], yp.at[half(c)], send_sem.at[base + 3], rsem, {"chaos": left}).start()

    def halo_arrived(which, i):
        c = source(i)
        pltpu.make_async_copy(xv.at[pl.ds(0, 96)], xv.at[pl.ds(0, 96)], halo_sem.at[which].at[c]).wait()

    def around(src, halo, c, r, h):
        xm, xp, ym, yp = halo
        at = pl.ds(al(c * 32 + r * SLOT + h * 8, 8), 8)
        other = pl.ds(al(c * 32 + (1 - r) * SLOT + h * 8, 8), 8)
        side = pl.ds(al(c * SLOT + h * 8, 8), 8)
        v = src[at, :]
        return (
            v,
            xm[at, :],
            xp[at, :],
            ym[side, :] if r == 0 else src[other, :],
            src[other, :] if r == 0 else yp[side, :],
            pltpu.roll(v, 1, 1),
            pltpu.roll(v, width - 1, 1),
        )

    scatter(xv, tv, 0)
    turn_in(f_ref, xf)
    tf[block(me), :] = xf[block(me), :]

    def send_source(i):
        @pl.when(i > 0)
        def _():
            c = target(i)
            remote(
                xf.at[block(c)], tf.at[block(me)], send_sem.at[5], a2a_sem.at[1].at[me], {"chaos": c}
            ).start()


    lane = lax.broadcasted_iota(jnp.int32, (1, width), 1)
    zm_mask = jnp.where(lane > 0, 0.5, 0.0).astype(F32)
    zp_mask = jnp.where(lane < width - 1, 0.5, 0.0).astype(F32)
    xm_mask = jnp.where(sp > 0, 0.5, 0.0).astype(F32)
    xp_mask = jnp.where(sp < space_n - 1, 0.5, 0.0).astype(F32)

    for copy in coef_copies:
        copy.wait()

    for r in range(2):
        y = me * 2 + r
        cn = cy[pl.ds(al(y * SLOT, SLOT), SLOT), :]
        cm = cy[pl.ds(al(lax.rem(y + rows - 1, rows) * SLOT, SLOT), SLOT), :]
        cp = cy[pl.ds(al(lax.rem(y + 1, rows) * SLOT, SLOT), SLOT), :]
        ym_mask = jnp.where(y > 0, 0.5, 0.0).astype(F32)
        yp_mask = jnp.where(y < rows - 1, 0.5, 0.0).astype(F32)
        total = 3.0 * cn
        near = (
            (cxm[pl.ds(r * SLOT, SLOT), :], xm_mask),
            (cxp[pl.ds(r * SLOT, SLOT), :], xp_mask),
            (cm, ym_mask),
            (cp, yp_mask),
            (pltpu.roll(cn, 1, 1), zm_mask),
            (pltpu.roll(cn, width - 1, 1), zp_mask),
        )
        for n, (other, mask) in enumerate(near):
            total = total + other * mask
            kf[pl.ds((r * 7 + n + 1) * SLOT, SLOT), :] = (cn + other) * mask
        kf[pl.ds(r * 7 * SLOT, SLOT), :] = total
    for r in range(2):
        for j in range(terms + 1):
            for n in range(7):
                row = kf[pl.ds((r * 7 + n) * SLOT + j, 1), :]
                kb[pl.ds(((r * (terms + 1) + j) * 7 + n) * 8, 8), :] = jnp.broadcast_to(row, (8, width))
        inv = 1.0 / kf[pl.ds(r * 7 * SLOT, 1), :]
        tb[pl.ds(r * 56 + 48, 8), :] = jnp.broadcast_to(inv, (8, width))
        for n in range(6):
            row = SECOND_COEF * kf[pl.ds((r * 7 + n + 1) * SLOT, 1), :] * inv
            tb[pl.ds(r * 56 + n * 8, 8), :] = jnp.broadcast_to(row, (8, width))

    c0 = cond_ref[0]
    yrow = lax.broadcasted_iota(jnp.int32, (rows, 1), 0)
    near = (
        (c0m[...], xm_mask),
        (c0p[...], xp_mask),
        (pltpu.roll(c0, 1, 0), jnp.where(yrow > 0, 0.5, 0.0).astype(F32)),
        (pltpu.roll(c0, rows - 1, 0), jnp.where(yrow < rows - 1, 0.5, 0.0).astype(F32)),
        (pltpu.roll(c0, 1, 1), zm_mask),
        (pltpu.roll(c0, width - 1, 1), zp_mask),
    )
    diagonal = 3.0 * c0
    for other, mask in near:
        diagonal = diagonal + other * mask
    inverse = 1.0 / diagonal
    oc[6] = inverse
    for n, (other, mask) in enumerate(near):
        oc[n] = SECOND_COEF * ((c0 + other) * mask) * inverse

    def spread(tile, carry):
        for n in range(7):
            group = oc[n, pl.ds(al(tile * 8, 8), 8), :]
            for i in range(8):
                at = al((tile * 56 + i * 7 + n) * 8, 8)
                ob[pl.ds(at, 8), :] = jnp.broadcast_to(group[i : i + 1, :], (8, width))
        return carry

    lax.fori_loop(0, tiles, spread, 0)

    def products(src, halo, which, y, i):
        halo_arrived(which, i)
        c = source(i)
        to = half(c)
        for r in range(2):
            for h in range(2):
                near = around(src, halo, c, r, h)
                for j in range(terms + 1):
                    base = (r * (terms + 1) + j) * 56
                    value = kb[pl.ds(base, 8), :] * near[0]
                    for n in range(1, 7):
                        value = value - kb[pl.ds(base + n * 8, 8), :] * near[n]
                    if j == 0:
                        y[pl.ds(al(c * 32 + r * SLOT + h * 8, 8), 8), :] = value
                    else:
                        acc[j - 1, pl.ds(h * 8, 8), :] = value
            for j in range(terms):
                value = acc[j, pl.ds(0, SLOT), :]
                top = value.astype(BF16)
                ph[j, to, pl.ds(r * width, width)] = top
                plo[j, to, pl.ds(r * width, width)] = (value - top.astype(F32)).astype(BF16)

    def mix(y):
        def body(j, total):
            a, b = (gh[j], ph[j])
            total = total + jnp.dot(a, b, preferred_element_type=F32)
            total = total + jnp.dot(a, plo[j], preferred_element_type=F32)
            return total + jnp.dot(gl[j], b, preferred_element_type=F32)

        total = lax.fori_loop(0, terms, body, jnp.zeros((slots, 2 * width), F32))
        for c in range(chaos_n):
            for r in range(2):
                at = pl.ds(c * 32 + r * SLOT, SLOT)
                y[at, :] = y[at, :] + total[c * SLOT : (c + 1) * SLOT, r * width : (r + 1) * width]

    index = lax.broadcasted_iota(jnp.int32, (slots, lists_ref.shape[-1]), 0).astype(F32)
    nt = (((1,), (1,)), ((), ()))

    def build(j, carry):
        first = lists_ref[pl.ds(j, 1), :]
        second = lists_ref[pl.ds(j + terms, 1), :]
        weight = lists_ref[pl.ds(j + 2 * terms, 1), :]
        weight_high = weight.astype(BF16).astype(F32)
        weight_low = weight - weight_high
        oa[...] = jnp.where(index == first, 1.0, 0.0).astype(BF16)
        here = index == second
        wh[...] = jnp.where(here, weight_high, 0.0).astype(BF16)
        wl[...] = jnp.where(here, weight_low, 0.0).astype(BF16)
        a, b, c = (oa[...], wh[...], wl[...])
        g = lax.dot_general(a, b, nt, preferred_element_type=F32)
        g = g + lax.dot_general(a, c, nt, preferred_element_type=F32)
        g = g + lax.dot_general(b, a, nt, preferred_element_type=F32)
        g = g + lax.dot_general(c, a, nt, preferred_element_type=F32)
        top = g.astype(BF16)
        gh[j] = top
        gl[j] = (g - top.astype(F32)).astype(BF16)

        def step(n, inner):
            i = j * per + n

            @pl.when(i < chaos_n)
            def _():
                arrived(tv, 0, i)
                spread_halo(tv, (vxm, vxp, vym, vyp), 0, i)
                send_source(i)

            @pl.when((i >= lag) & (i < chaos_n))
            def _():
                products(tv, (vxm, vxp, vym, vyp), 0, y0, i - lag)

            return inner

        return lax.fori_loop(0, per, step, carry)

    lax.fori_loop(0, terms, build, 0)

    def rest(i, carry):
        products(tv, (vxm, vxp, vym, vyp), 0, y0, i)
        return carry

    lax.fori_loop(chaos_n - lag, chaos_n, rest, 0)
    mix(y0)

    sums[...] = jnp.zeros_like(sums)

    def weigh(row, value):
        sums[pl.ds(row * 8, 8), :] = sums[pl.ds(row * 8, 8), :] + value

    def residual_step(i):
        arrived(tf, 1, i)
        c = source(i)
        for r in range(2):
            inv = tb[pl.ds(r * 56 + 48, 8), :]
            for h in range(2):
                at = pl.ds(al(c * 32 + r * SLOT + h * 8, 8), 8)
                value = tf[at, :] - y0[at, :]
                tr[at, :] = value
                tz[at, :] = value * inv
        spread_halo(tz, (zxm, zxp, zym, zyp), 1, i)

        @pl.when(i > 0)
        def _():
            remote(
                tr.at[block(c)], rr.at[block(me)], send_sem.at[6], a2a_sem.at[2].at[me], {"chaos": c}
            ).start()

    def search_step(i):
        halo_arrived(1, i)
        c = source(i)
        for r in range(2):
            coef = [tb[pl.ds(r * 56 + n * 8, 8), :] for n in range(6)]
            for h in range(2):
                at = pl.ds(al(c * 32 + r * SLOT + h * 8, 8), 8)
                near = around(tz, (zxm, zxp, zym, zyp), c, r, h)
                value = (FIRST_COEF - SECOND_COEF) * near[0]
                for n in range(6):
                    value = value + coef[n] * near[n + 1]
                ts[at, :] = value
                weigh(0, value * tr[at, :])
        spread_halo(ts, (sxm, sxp, sym, syp), 2, i)

    def each(step):
        def body(i, carry):
            step(i)
            return carry

        lax.fori_loop(0, chaos_n, body, 0)

    each(residual_step)
    each(search_step)
    each(lambda i: products(ts, (sxm, sxp, sym, syp), 2, y1, i))
    rr[block(me), :] = tr[block(me), :]
    mix(y1)
    scatter(y1, qq, 3)

    def image_step(i, carry):
        c = source(i)
        for r in range(2):
            inv = tb[pl.ds(r * 56 + 48, 8), :]
            for h in range(2):
                at = pl.ds(al(c * 32 + r * SLOT + h * 8, 8), 8)
                tw[at, :] = y1[at, :] * inv
        spread_halo(tw, (wxm, wxp, wym, wyp), 3, i)
        return carry

    lax.fori_loop(0, chaos_n, image_step, 0)

    def slab_step(src, which, z, zm, zp, base, number):
        def body(i, carry):
            arrived(src, which, i)
            c = source(i)
            for r in range(2):
                inv = ob[pl.ds(al((c * 2 + r) * 56 + 48, 8), 8), :]
                for h in range(2):
                    at = pl.ds(al(c * 32 + r * SLOT + h * 8, 8), 8)
                    z[at, :] = src[at, :] * inv
            rsem = slab_sem.at[number].at[c]
            remote(z.at[block(c)], zm.at[block(c)], send_sem.at[base], rsem, {"space": up}).start()
            remote(z.at[block(c)], zp.at[block(c)], send_sem.at[base + 1], rsem, {"space": down}).start()
            return carry

        lax.fori_loop(0, chaos_n, body, 0)

    def slab_finish(z, zm, zp, number, to):
        def body(i, carry):
            c = source(i)
            pltpu.make_async_copy(xv.at[pl.ds(0, 64)], xv.at[pl.ds(0, 64)], slab_sem.at[number].at[c]).wait()
            for r in range(2):
                line = c * 2 + r
                prev = lax.rem(line + rows - 1, rows)
                after = lax.rem(line + 1, rows)
                coef = [ob[pl.ds(al(line * 56 + n * 8, 8), 8), :] for n in range(6)]
                for h in range(2):
                    at = pl.ds(al(line * SLOT + h * 8, 8), 8)
                    v = z[at, :]
                    near = (
                        zm[at, :],
                        zp[at, :],
                        z[pl.ds(al(prev * SLOT + h * 8, 8), 8), :],
                        z[pl.ds(al(after * SLOT + h * 8, 8), 8), :],
                        pltpu.roll(v, 1, 1),
                        pltpu.roll(v, width - 1, 1),
                    )
                    value = (FIRST_COEF - SECOND_COEF) * v
                    for n in range(6):
                        value = value + coef[n] * near[n]
                    to[at, :] = value
            return carry

        lax.fori_loop(0, chaos_n, body, 0)

    slab_step(rr, 2, zr, zrm, zrp, 24, 0)

    def image_dot(i, carry):
        halo_arrived(3, i)
        c = source(i)
        for r in range(2):
            coef = [tb[pl.ds(r * 56 + n * 8, 8), :] for n in range(6)]
            for h in range(2):
                at = pl.ds(al(c * 32 + r * SLOT + h * 8, 8), 8)
                near = around(tw, (wxm, wxp, wym, wyp), c, r, h)
                value = (FIRST_COEF - SECOND_COEF) * near[0]
                for n in range(6):
                    value = value + coef[n] * near[n + 1]
                image = y1[at, :]
                weigh(1, image * ts[at, :])
                weigh(2, image * value)
        return carry

    lax.fori_loop(0, chaos_n, image_dot, 0)
    dots[...] = blank
    for n in range(3):
        dots[pl.ds(n, 1), :] = jnp.sum(sums[pl.ds(n * 8, 8), :], axis=0, keepdims=True)

    def tell(k, carry):
        c = lax.rem(me + k, chaos_n)
        remote(dots, dga.at[k], send_sem.at[28], dota_sem.at[k], {"chaos": c}).start()
        return carry

    lax.fori_loop(1, chaos_n, tell, 0)

    slab_finish(zr, zrm, zrp, 0, ss)

    slab_step(qq, 3, zq, zqm, zqp, 26, 1)

    def hear(k, total):
        remote(dots, dga.at[k], send_sem.at[28], dota_sem.at[k], {"chaos": left}).wait_recv()
        return total + dga[k]

    dsum[...] = lax.fori_loop(1, chaos_n, hear, dots[...])

    def tell_space(k, carry):
        there = lax.rem(sp + k, space_n)
        remote(dsum, dgb.at[k], send_sem.at[29], dotb_sem.at[k], {"space": there}).start()
        return carry

    lax.fori_loop(1, space_n, tell_space, 0)

    slab_finish(zq, zqm, zqp, 1, mq)

    def hear_space(k, total):
        remote(dsum, dgb.at[k], send_sem.at[29], dotb_sem.at[k], {"space": up}).wait_recv()
        return total + dgb[k]

    whole = lax.fori_loop(1, space_n, hear_space, dsum[...])
    lanes = jnp.sum(whole, axis=1, keepdims=True)
    energy_start, curvature, image_energy = (lanes[0:1, :], lanes[1:2, :], lanes[2:3, :])
    step_size = energy_start / curvature
    energy_next = energy_start - 2.0 * step_size * curvature + step_size * step_size * image_energy
    ratio = 1.0 + energy_next / energy_start
    step_all = jnp.broadcast_to(step_size, (8, width))
    ratio_all = jnp.broadcast_to(ratio, (8, width))

    def turn_out(m, carry):
        for tile in range(tiles):
            where = pl.ds(tile * 128 + m, 8, stride=SLOT)
            there = pl.ds(tile * 8, 8)
            search = ss[where, :]
            sol_ref[m, there, :] = v_ref[m, there, :] + step_all * search
            res_ref[m, there, :] = rr[where, :] - step_all * qq[where, :]
            dir_ref[m, there, :] = ratio_all * search - step_all * mq[where, :]
        return carry

    lax.fori_loop(0, own_modes, turn_out, 0)

    for n, ref in enumerate((xv, xf, tr, y1)):
        drain(ref, (chaos_n - 1) * 32, send_sem.at[4 + n])
    for n, ref in enumerate((tv, tz, ts, tw)):
        for m, count in enumerate((flat, flat, flat // 2, flat // 2)):
            drain(ref, count, send_sem.at[8 + n * 4 + m])
    for n, ref in enumerate((zr, zq)):
        for m in range(2):
            drain(ref, flat, send_sem.at[24 + n * 2 + m])
    pltpu.make_async_copy(dga.at[pl.ds(1, chaos_n - 1)], dga.at[pl.ds(1, chaos_n - 1)], send_sem.at[28]).wait()
    pltpu.make_async_copy(dgb.at[pl.ds(1, space_n - 1)], dgb.at[pl.ds(1, space_n - 1)], send_sem.at[29]).wait()


def per_device(chaos_n, space_n, source_term, start_field, conductivity, pair_modes, pair_weight):
    own_modes, _, rows, width = source_term.shape
    terms, pairs = pair_weight.shape
    slots = chaos_n * SLOT
    flat = rows * SLOT
    padded = -(-pairs // 128) * 128
    ends = pair_modes + pair_modes // own_modes * (SLOT - own_modes)
    lists = jnp.concatenate(
        [ends[:, :, 0].astype(F32), ends[:, :, 1].astype(F32), pair_weight], axis=0
    )
    lists = jnp.pad(lists, ((0, 0), (0, padded - pairs)), constant_values=-1.0)
    field = pltpu.VMEM((flat, width), F32)
    half = pltpu.VMEM((flat // 2, width), F32)
    vmem = pl.BlockSpec(memory_space=pltpu.VMEM)
    shape = jax.ShapeDtypeStruct((own_modes, rows, width), F32)
    outs = pl.pallas_call(
        functools.partial(kernel, chaos_n, space_n, terms, own_modes, rows),
        out_shape=(shape, shape, shape),
        in_specs=[vmem] * 4,
        out_specs=(vmem, vmem, vmem),
        scratch_shapes=[field] * 28
        + [half] * 8
        + [field]
        + [pltpu.VMEM((32, width), F32)] * 2
        + [pltpu.VMEM((rows, width), F32)] * 2
        + [
            pltpu.VMEM((7, rows, width), F32),
            pltpu.VMEM((rows * 56, width), F32),
            pltpu.VMEM((14 * SLOT, width), F32),
            pltpu.VMEM((2 * (terms + 1) * 56, width), F32),
            pltpu.VMEM((112, width), F32),
            pltpu.VMEM((terms, slots, slots), BF16),
            pltpu.VMEM((terms, slots, slots), BF16),
            pltpu.VMEM((slots, padded), BF16),
            pltpu.VMEM((slots, padded), BF16),
            pltpu.VMEM((slots, padded), BF16),
            pltpu.VMEM((terms, slots, 2 * width), BF16),
            pltpu.VMEM((terms, slots, 2 * width), BF16),
            pltpu.VMEM((terms, SLOT, width), F32),
            pltpu.VMEM((24, width), F32),
            pltpu.VMEM((8, width), F32),
            pltpu.VMEM((8, width), F32),
            pltpu.VMEM((chaos_n, 8, width), F32),
            pltpu.VMEM((space_n, 8, width), F32),
            pltpu.SemaphoreType.DMA((4,)),
            pltpu.SemaphoreType.DMA((30,)),
            pltpu.SemaphoreType.DMA((4, chaos_n)),
            pltpu.SemaphoreType.DMA((4, chaos_n)),
            pltpu.SemaphoreType.DMA((2, chaos_n)),
            pltpu.SemaphoreType.DMA((chaos_n,)),
            pltpu.SemaphoreType.DMA((space_n,)),
        ],
        compiler_params=pltpu.CompilerParams(
            collective_id=0, has_side_effects=True, vmem_limit_bytes=60 * 1024 * 1024
        ),
    )(
        start_field.reshape(own_modes, rows, width),
        source_term.reshape(own_modes, rows, width),
        conductivity.reshape(terms + 1, rows, width),
        lists,
    )
    return tuple(out.reshape(source_term.shape) for out in outs)


def solution(mesh):
    chaos_n, space_n = (mesh.shape["chaos"], mesh.shape["space"])
    field = P("chaos", "space", None, None)
    return jax.shard_map(
        functools.partial(per_device, chaos_n, space_n),
        mesh=mesh,
        in_specs=(field, field, P(None, "space", None, None), P(), P()),
        out_specs=(field, field, field),
        check_vma=False,
    )
```

```python
import functools

import jax
import jax.numpy as jnp
from jax import lax
from jax.experimental import pallas as pl
from jax.experimental.pallas import tpu as pltpu
from jax.sharding import PartitionSpec as P

CENTER_BOUND = 1.05
HALF_WIDTH = 0.95
FIRST_COEF = 4.0 * CENTER_BOUND / (2.0 * CENTER_BOUND * CENTER_BOUND - HALF_WIDTH * HALF_WIDTH)
SECOND_COEF = 2.0 / (2.0 * CENTER_BOUND * CENTER_BOUND - HALF_WIDTH * HALF_WIDTH)
SLOT = 16
F32 = jnp.float32
BF16 = jnp.bfloat16
MESH = pl.DeviceIdType.MESH


def al(value, unit):
    return pl.multiple_of(value, unit)


def kernel(
    chaos_n, space_n, terms, own_modes, rows,
    v_ref, f_ref, cond_ref, lists_ref,
    ss, mq, rr_ref, qq_ref, scale_ref,
    xv, xf, rr, qq, zr, zrm, zrp, zq, zqm, zqp,
    tv, tf, tr, tz, ts, tw, y0, y1,
    vxm, vxp, zxm, zxp, sxm, sxp, wxm, wxp,
    vym, vyp, zym, zyp, sym, syp, wym, wyp,
    cy, cxm, cxp, c0m, c0p, oc, ob, kf, kb, tb,
    gh, gl, oa, wh, wl, ph, plo, acc,
    sums, dots, dsum, dga, dgb,
    coef_sem, send_sem, a2a_sem, halo_sem, slab_sem, dota_sem, dotb_sem,
):
    me = lax.axis_index("chaos")
    sp = lax.axis_index("space")
    up = lax.rem(sp + 1, space_n)
    down = lax.rem(sp + space_n - 1, space_n)
    right = lax.rem(me + 1, chaos_n)
    left = lax.rem(me + chaos_n - 1, chaos_n)
    slots = chaos_n * SLOT
    flat = rows * SLOT
    width = v_ref.shape[-1]
    tiles = rows // 8
    per = -(-chaos_n // terms)
    lag = max(2, chaos_n // 2)

    def swing(i):
        return (2 * lax.rem(i, 2) - 1) * ((i + 1) // 2)

    def target(i):
        return lax.rem(me + chaos_n + swing(i), chaos_n)

    def source(i):
        return lax.rem(me + chaos_n - swing(i), chaos_n)

    def block(c):
        return pl.ds(al(c * 32, 32), 32)

    def low(c):
        return pl.ds(al(c * 32, 32), SLOT)

    def high(c):
        return pl.ds(al(c * 32 + SLOT, SLOT), SLOT)

    def half(c):
        return pl.ds(al(c * SLOT, SLOT), SLOT)

    def remote(src, dst, ssem, rsem, device):
        return pltpu.make_async_remote_copy(
            src_ref=src, dst_ref=dst, send_sem=ssem, recv_sem=rsem,
            device_id=device, device_id_type=MESH,
        )

    def drain(ref, count, sem):
        pltpu.make_async_copy(ref.at[pl.ds(0, count)], ref.at[pl.ds(0, count)], sem).wait()

    barrier = pltpu.get_barrier_semaphore()

    def greet_chaos(k, carry):
        pl.semaphore_signal(
            barrier, inc=1, device_id={"chaos": lax.rem(me + k, chaos_n)}, device_id_type=MESH
        )
        return carry

    lax.fori_loop(1, chaos_n, greet_chaos, 0)

    def greet_space(k, carry):
        pl.semaphore_signal(
            barrier, inc=1, device_id={"space": lax.rem(sp + k, space_n)}, device_id_type=MESH
        )
        return carry

    lax.fori_loop(1, space_n, greet_space, 0)

    blank = jnp.zeros((8, width), F32)

    def turn_in(from_ref, to_ref):
        def body(m, carry):
            for tile in range(tiles):
                to_ref[pl.ds(tile * 128 + m, 8, stride=SLOT), :] = from_ref[m, pl.ds(tile * 8, 8), :]
            return carry

        lax.fori_loop(0, own_modes, body, 0)
        for m in range(own_modes, SLOT):
            for tile in range(tiles):
                to_ref[pl.ds(tile * 128 + m, 8, stride=SLOT), :] = blank

    turn_in(v_ref, xv)
    for j in range(SLOT):
        for tile in range(tiles):
            value = cond_ref[j, pl.ds(tile * 8, 8), :] if j <= terms else blank
            cy[pl.ds(tile * 128 + j, 8, stride=SLOT), :] = value

    pl.semaphore_wait(barrier, chaos_n - 1 + space_n - 1)

    coef_copies = (
        remote(cy.at[block(me)], cxm.at[pl.ds(0, 32)], send_sem.at[0], coef_sem.at[0], {"space": up}),
        remote(cy.at[block(me)], cxp.at[pl.ds(0, 32)], send_sem.at[1], coef_sem.at[1], {"space": down}),
        remote(cond_ref.at[0], c0m, send_sem.at[2], coef_sem.at[2], {"space": up}),
        remote(cond_ref.at[0], c0p, send_sem.at[3], coef_sem.at[3], {"space": down}),
    )
    for copy in coef_copies:
        copy.start()

    def scatter(src, dst, which):
        def body(i, carry):
            c = target(i)
            remote(
                src.at[block(c)], dst.at[block(me)], send_sem.at[4 + which], a2a_sem.at[which].at[me], {"chaos": c}
            ).start()
            return carry

        lax.fori_loop(1, chaos_n, body, 0)
        dst[block(me), :] = src[block(me), :]

    def arrived(dst, which, i):
        @pl.when(i > 0)
        def _():
            c = source(i)
            remote(
                dst.at[block(c)], dst.at[block(c)], send_sem.at[4], a2a_sem.at[which].at[c], {"chaos": left}
            ).wait_recv()

    def spread_halo(src, halo, which, i):
        c = source(i)
        xm, xp, ym, yp = halo
        rsem = halo_sem.at[which].at[c]
        base = 8 + which * 4
        remote(src.at[block(c)], xm.at[block(c)], send_sem.at[base], rsem, {"space": up}).start()
        remote(src.at[block(c)], xp.at[block(c)], send_sem.at[base + 1], rsem, {"space": down}).start()
        remote(src.at[high(c)], ym.at[half(c)], send_sem.at[base + 2], rsem, {"chaos": right}).start()
        remote(src.at[low(c)], yp.at[half(c)], send_sem.at[base + 3], rsem, {"chaos": left}).start()

    def halo_arrived(which, i):
        c = source(i)
        pltpu.make_async_copy(xv.at[pl.ds(0, 96)], xv.at[pl.ds(0, 96)], halo_sem.at[which].at[c]).wait()

    def around(src, halo, c, r, h):
        xm, xp, ym, yp = halo
        at = pl.ds(al(c * 32 + r * SLOT + h * 8, 8), 8)
        other = pl.ds(al(c * 32 + (1 - r) * SLOT + h * 8, 8), 8)
        side = pl.ds(al(c * SLOT + h * 8, 8), 8)
        v = src[at, :]
        return (
            v,
            xm[at, :],
            xp[at, :],
            ym[side, :] if r == 0 else src[other, :],
            src[other, :] if r == 0 else yp[side, :],
            pltpu.roll(v, 1, 1),
            pltpu.roll(v, width - 1, 1),
        )

    scatter(xv, tv, 0)
    turn_in(f_ref, xf)
    tf[block(me), :] = xf[block(me), :]

    def send_source(i):
        @pl.when(i > 0)
        def _():
            c = target(i)
            remote(
                xf.at[block(c)], tf.at[block(me)], send_sem.at[5], a2a_sem.at[1].at[me], {"chaos": c}
            ).start()


    lane = lax.broadcasted_iota(jnp.int32, (1, width), 1)
    zm_mask = jnp.where(lane > 0, 0.5, 0.0).astype(F32)
    zp_mask = jnp.where(lane < width - 1, 0.5, 0.0).astype(F32)
    xm_mask = jnp.where(sp > 0, 0.5, 0.0).astype(F32)
    xp_mask = jnp.where(sp < space_n - 1, 0.5, 0.0).astype(F32)

    for copy in coef_copies:
        copy.wait()

    for r in range(2):
        y = me * 2 + r
        cn = cy[pl.ds(al(y * SLOT, SLOT), SLOT), :]
        cm = cy[pl.ds(al(lax.rem(y + rows - 1, rows) * SLOT, SLOT), SLOT), :]
        cp = cy[pl.ds(al(lax.rem(y + 1, rows) * SLOT, SLOT), SLOT), :]
        ym_mask = jnp.where(y > 0, 0.5, 0.0).astype(F32)
        yp_mask = jnp.where(y < rows - 1, 0.5, 0.0).astype(F32)
        total = 3.0 * cn
        near = (
            (cxm[pl.ds(r * SLOT, SLOT), :], xm_mask),
            (cxp[pl.ds(r * SLOT, SLOT), :], xp_mask),
            (cm, ym_mask),
            (cp, yp_mask),
            (pltpu.roll(cn, 1, 1), zm_mask),
            (pltpu.roll(cn, width - 1, 1), zp_mask),
        )
        for n, (other, mask) in enumerate(near):
            total = total + other * mask
            kf[pl.ds((r * 7 + n + 1) * SLOT, SLOT), :] = (cn + other) * mask
        kf[pl.ds(r * 7 * SLOT, SLOT), :] = total
    for r in range(2):
        for j in range(terms + 1):
            for n in range(7):
                row = kf[pl.ds((r * 7 + n) * SLOT + j, 1), :]
                kb[pl.ds(((r * (terms + 1) + j) * 7 + n) * 8, 8), :] = jnp.broadcast_to(row, (8, width))
        inv = 1.0 / kf[pl.ds(r * 7 * SLOT, 1), :]
        tb[pl.ds(r * 56 + 48, 8), :] = jnp.broadcast_to(inv, (8, width))
        for n in range(6):
            row = SECOND_COEF * kf[pl.ds((r * 7 + n + 1) * SLOT, 1), :] * inv
            tb[pl.ds(r * 56 + n * 8, 8), :] = jnp.broadcast_to(row, (8, width))

    c0 = cond_ref[0]
    yrow = lax.broadcasted_iota(jnp.int32, (rows, 1), 0)
    near = (
        (c0m[...], xm_mask),
        (c0p[...], xp_mask),
        (pltpu.roll(c0, 1, 0), jnp.where(yrow > 0, 0.5, 0.0).astype(F32)),
        (pltpu.roll(c0, rows - 1, 0), jnp.where(yrow < rows - 1, 0.5, 0.0).astype(F32)),
        (pltpu.roll(c0, 1, 1), zm_mask),
        (pltpu.roll(c0, width - 1, 1), zp_mask),
    )
    diagonal = 3.0 * c0
    for other, mask in near:
        diagonal = diagonal + other * mask
    inverse = 1.0 / diagonal
    oc[6] = inverse
    for n, (other, mask) in enumerate(near):
        oc[n] = SECOND_COEF * ((c0 + other) * mask) * inverse

    def spread(tile, carry):
        for n in range(7):
            group = oc[n, pl.ds(al(tile * 8, 8), 8), :]
            for i in range(8):
                at = al((tile * 56 + i * 7 + n) * 8, 8)
                ob[pl.ds(at, 8), :] = jnp.broadcast_to(group[i : i + 1, :], (8, width))
        return carry

    lax.fori_loop(0, tiles, spread, 0)

    def products(src, halo, which, y, i):
        halo_arrived(which, i)
        c = source(i)
        to = half(c)
        for r in range(2):
            for h in range(2):
                near = around(src, halo, c, r, h)
                for j in range(terms + 1):
                    base = (r * (terms + 1) + j) * 56
                    value = kb[pl.ds(base, 8), :] * near[0]
                    for n in range(1, 7):
                        value = value - kb[pl.ds(base + n * 8, 8), :] * near[n]
                    if j == 0:
                        y[pl.ds(al(c * 32 + r * SLOT + h * 8, 8), 8), :] = value
                    else:
                        acc[j - 1, pl.ds(h * 8, 8), :] = value
            for j in range(terms):
                value = acc[j, pl.ds(0, SLOT), :]
                top = value.astype(BF16)
                ph[j, to, pl.ds(r * width, width)] = top
                plo[j, to, pl.ds(r * width, width)] = (value - top.astype(F32)).astype(BF16)

    def mix(y):
        def body(j, total):
            a, b = (gh[j], ph[j])
            total = total + jnp.dot(a, b, preferred_element_type=F32)
            total = total + jnp.dot(a, plo[j], preferred_element_type=F32)
            return total + jnp.dot(gl[j], b, preferred_element_type=F32)

        total = lax.fori_loop(0, terms, body, jnp.zeros((slots, 2 * width), F32))
        for c in range(chaos_n):
            for r in range(2):
                at = pl.ds(c * 32 + r * SLOT, SLOT)
                y[at, :] = y[at, :] + total[c * SLOT : (c + 1) * SLOT, r * width : (r + 1) * width]

    index = lax.broadcasted_iota(jnp.int32, (slots, lists_ref.shape[-1]), 0).astype(F32)
    nt = (((1,), (1,)), ((), ()))

    def build(j, carry):
        first = lists_ref[pl.ds(j, 1), :]
        second = lists_ref[pl.ds(j + terms, 1), :]
        first = first + (SLOT - own_modes) * jnp.floor((first + 0.5) * (1.0 / own_modes))
        second = second + (SLOT - own_modes) * jnp.floor((second + 0.5) * (1.0 / own_modes))
        weight = lists_ref[pl.ds(j + 2 * terms, 1), :]
        weight_high = weight.astype(BF16).astype(F32)
        weight_low = weight - weight_high
        oa[...] = jnp.where(index == first, 1.0, 0.0).astype(BF16)
        here = index == second
        wh[...] = jnp.where(here, weight_high, 0.0).astype(BF16)
        wl[...] = jnp.where(here, weight_low, 0.0).astype(BF16)
        a, b, c = (oa[...], wh[...], wl[...])
        g = lax.dot_general(a, b, nt, preferred_element_type=F32)
        g = g + lax.dot_general(a, c, nt, preferred_element_type=F32)
        g = g + lax.dot_general(b, a, nt, preferred_element_type=F32)
        g = g + lax.dot_general(c, a, nt, preferred_element_type=F32)
        top = g.astype(BF16)
        gh[j] = top
        gl[j] = (g - top.astype(F32)).astype(BF16)

        def step(n, inner):
            i = j * per + n

            @pl.when(i < chaos_n)
            def _():
                arrived(tv, 0, i)
                spread_halo(tv, (vxm, vxp, vym, vyp), 0, i)
                send_source(i)

            @pl.when((i >= lag) & (i < chaos_n))
            def _():
                products(tv, (vxm, vxp, vym, vyp), 0, y0, i - lag)

            return inner

        return lax.fori_loop(0, per, step, carry)

    lax.fori_loop(0, terms, build, 0)

    def rest(i, carry):
        products(tv, (vxm, vxp, vym, vyp), 0, y0, i)
        return carry

    lax.fori_loop(chaos_n - lag, chaos_n, rest, 0)
    mix(y0)

    sums[...] = jnp.zeros_like(sums)

    def weigh(row, value):
        sums[pl.ds(row * 8, 8), :] = sums[pl.ds(row * 8, 8), :] + value

    def residual_step(i):
        arrived(tf, 1, i)
        c = source(i)
        for r in range(2):
            inv = tb[pl.ds(r * 56 + 48, 8), :]
            for h in range(2):
                at = pl.ds(al(c * 32 + r * SLOT + h * 8, 8), 8)
                value = tf[at, :] - y0[at, :]
                tr[at, :] = value
                tz[at, :] = value * inv
        spread_halo(tz, (zxm, zxp, zym, zyp), 1, i)

    def search_step(i):
        halo_arrived(1, i)
        c = source(i)
        for r in range(2):
            coef = [tb[pl.ds(r * 56 + n * 8, 8), :] for n in range(6)]
            for h in range(2):
                at = pl.ds(al(c * 32 + r * SLOT + h * 8, 8), 8)
                near = around(tz, (zxm, zxp, zym, zyp), c, r, h)
                value = (FIRST_COEF - SECOND_COEF) * near[0]
                for n in range(6):
                    value = value + coef[n] * near[n + 1]
                ts[at, :] = value
                weigh(0, value * tr[at, :])
        spread_halo(ts, (sxm, sxp, sym, syp), 2, i)

    def each(step):
        def body(i, carry):
            step(i)
            return carry

        lax.fori_loop(0, chaos_n, body, 0)

    each(residual_step)
    each(search_step)

    def last_step(i):
        c = source(i)

        @pl.when(i > 0)
        def _():
            remote(
                tr.at[block(c)], rr.at[block(me)], send_sem.at[6], a2a_sem.at[2].at[me], {"chaos": c}
            ).start()

        products(ts, (sxm, sxp, sym, syp), 2, y1, i)

    each(last_step)
    rr[block(me), :] = tr[block(me), :]
    mix(y1)
    scatter(y1, qq, 3)

    def image_step(i, carry):
        c = source(i)
        for r in range(2):
            inv = tb[pl.ds(r * 56 + 48, 8), :]
            for h in range(2):
                at = pl.ds(al(c * 32 + r * SLOT + h * 8, 8), 8)
                tw[at, :] = y1[at, :] * inv
        spread_halo(tw, (wxm, wxp, wym, wyp), 3, i)
        return carry

    lax.fori_loop(0, chaos_n, image_step, 0)

    def slab_step(src, which, z, zm, zp, base, number):
        def body(i, carry):
            arrived(src, which, i)
            c = source(i)
            for r in range(2):
                inv = ob[pl.ds(al((c * 2 + r) * 56 + 48, 8), 8), :]
                for h in range(2):
                    at = pl.ds(al(c * 32 + r * SLOT + h * 8, 8), 8)
                    z[at, :] = src[at, :] * inv
            rsem = slab_sem.at[number].at[c]
            remote(z.at[block(c)], zm.at[block(c)], send_sem.at[base], rsem, {"space": up}).start()
            remote(z.at[block(c)], zp.at[block(c)], send_sem.at[base + 1], rsem, {"space": down}).start()
            return carry

        lax.fori_loop(0, chaos_n, body, 0)

    def slab_finish(z, zm, zp, number, to, field, keep):
        def body(i, carry):
            c = source(i)
            pltpu.make_async_copy(xv.at[pl.ds(0, 64)], xv.at[pl.ds(0, 64)], slab_sem.at[number].at[c]).wait()
            for r in range(2):
                line = c * 2 + r
                prev = lax.rem(line + rows - 1, rows)
                after = lax.rem(line + 1, rows)
                coef = [ob[pl.ds(al(line * 56 + n * 8, 8), 8), :] for n in range(6)]
                for h in range(2):
                    at = pl.ds(al(line * SLOT + h * 8, 8), 8)
                    v = z[at, :]
                    near = (
                        zm[at, :],
                        zp[at, :],
                        z[pl.ds(al(prev * SLOT + h * 8, 8), 8), :],
                        z[pl.ds(al(after * SLOT + h * 8, 8), 8), :],
                        pltpu.roll(v, 1, 1),
                        pltpu.roll(v, width - 1, 1),
                    )
                    value = (FIRST_COEF - SECOND_COEF) * v
                    for n in range(6):
                        value = value + coef[n] * near[n]
                    to[at, :] = value
                    keep[at, :] = field[at, :]
            return carry

        lax.fori_loop(0, chaos_n, body, 0)

    slab_step(rr, 2, zr, zrm, zrp, 24, 0)

    def image_dot(i, carry):
        halo_arrived(3, i)
        c = source(i)
        for r in range(2):
            coef = [tb[pl.ds(r * 56 + n * 8, 8), :] for n in range(6)]
            for h in range(2):
                at = pl.ds(al(c * 32 + r * SLOT + h * 8, 8), 8)
                near = around(tw, (wxm, wxp, wym, wyp), c, r, h)
                value = (FIRST_COEF - SECOND_COEF) * near[0]
                for n in range(6):
                    value = value + coef[n] * near[n + 1]
                image = y1[at, :]
                weigh(1, image * ts[at, :])
                weigh(2, image * value)
        return carry

    lax.fori_loop(0, chaos_n, image_dot, 0)
    dots[...] = blank
    for n in range(3):
        dots[pl.ds(n, 1), :] = jnp.sum(sums[pl.ds(n * 8, 8), :], axis=0, keepdims=True)

    def tell(k, carry):
        c = lax.rem(me + k, chaos_n)
        remote(dots, dga.at[k], send_sem.at[28], dota_sem.at[k], {"chaos": c}).start()
        return carry

    lax.fori_loop(1, chaos_n, tell, 0)

    slab_finish(zr, zrm, zrp, 0, ss, rr, rr_ref)

    slab_step(qq, 3, zq, zqm, zqp, 26, 1)

    def hear(k, total):
        remote(dots, dga.at[k], send_sem.at[28], dota_sem.at[k], {"chaos": left}).wait_recv()
        return total + dga[k]

    dsum[...] = lax.fori_loop(1, chaos_n, hear, dots[...])

    def tell_space(k, carry):
        there = lax.rem(sp + k, space_n)
        remote(dsum, dgb.at[k], send_sem.at[29], dotb_sem.at[k], {"space": there}).start()
        return carry

    lax.fori_loop(1, space_n, tell_space, 0)

    slab_finish(zq, zqm, zqp, 1, mq, qq, qq_ref)

    def hear_space(k, total):
        remote(dsum, dgb.at[k], send_sem.at[29], dotb_sem.at[k], {"space": up}).wait_recv()
        return total + dgb[k]

    whole = lax.fori_loop(1, space_n, hear_space, dsum[...])
    lanes = jnp.sum(whole, axis=1, keepdims=True)
    energy_start, curvature, image_energy = (lanes[0:1, :], lanes[1:2, :], lanes[2:3, :])
    step_size = energy_start / curvature
    energy_next = energy_start - 2.0 * step_size * curvature + step_size * step_size * image_energy
    ratio = 1.0 + energy_next / energy_start
    scale_ref[pl.ds(0, 8), :] = jnp.broadcast_to(step_size, (8, width))
    scale_ref[pl.ds(8, 8), :] = jnp.broadcast_to(ratio, (8, width))

    for n, ref in enumerate((xv, xf, tr, y1)):
        drain(ref, (chaos_n - 1) * 32, send_sem.at[4 + n])
    for n, ref in enumerate((tv, tz, ts, tw)):
        for m, count in enumerate((flat, flat, flat // 2, flat // 2)):
            drain(ref, count, send_sem.at[8 + n * 4 + m])
    for n, ref in enumerate((zr, zq)):
        for m in range(2):
            drain(ref, flat, send_sem.at[24 + n * 2 + m])
    pltpu.make_async_copy(dga.at[pl.ds(1, chaos_n - 1)], dga.at[pl.ds(1, chaos_n - 1)], send_sem.at[28]).wait()
    pltpu.make_async_copy(dgb.at[pl.ds(1, space_n - 1)], dgb.at[pl.ds(1, space_n - 1)], send_sem.at[29]).wait()


def combine(own_modes, v_ref, ss, rr, qq, mq, scale_ref, sol_ref, res_ref, dir_ref):
    step_all = scale_ref[pl.ds(0, 8), :]
    ratio_all = scale_ref[pl.ds(8, 8), :]
    tiles = v_ref.shape[1] // 8

    def turn_out(m, carry):
        for tile in range(tiles):
            where = pl.ds(tile * 128 + m, 8, stride=SLOT)
            there = pl.ds(tile * 8, 8)
            search = ss[where, :]
            sol_ref[m, there, :] = v_ref[m, there, :] + step_all * search
            res_ref[m, there, :] = rr[where, :] - step_all * qq[where, :]
            dir_ref[m, there, :] = ratio_all * search - step_all * mq[where, :]
        return carry

    lax.fori_loop(0, own_modes, turn_out, 0)


def per_device(chaos_n, space_n, source_term, start_field, conductivity, pair_modes, pair_weight):
    own_modes, _, rows, width = source_term.shape
    terms, pairs = pair_weight.shape
    slots = chaos_n * SLOT
    flat = rows * SLOT
    padded = -(-pairs // 128) * 128
    lists = jnp.concatenate(
        [pair_modes[:, :, 0].astype(F32), pair_modes[:, :, 1].astype(F32), pair_weight], axis=0
    )
    lists = jnp.pad(lists, ((0, 0), (0, padded - pairs)), constant_values=-1.0)
    field = pltpu.VMEM((flat, width), F32)
    half = pltpu.VMEM((flat // 2, width), F32)
    vmem = pl.BlockSpec(memory_space=pltpu.VMEM)
    shape = jax.ShapeDtypeStruct((own_modes, rows, width), F32)
    flat_shape = jax.ShapeDtypeStruct((flat, width), F32)
    start = start_field.reshape(own_modes, rows, width)
    search, precond, residual, image, scale = pl.pallas_call(
        functools.partial(kernel, chaos_n, space_n, terms, own_modes, rows),
        out_shape=(flat_shape,) * 4 + (jax.ShapeDtypeStruct((16, width), F32),),
        in_specs=[vmem] * 4,
        out_specs=(vmem,) * 5,
        scratch_shapes=[field] * 26
        + [half] * 8
        + [field]
        + [pltpu.VMEM((32, width), F32)] * 2
        + [pltpu.VMEM((rows, width), F32)] * 2
        + [
            pltpu.VMEM((7, rows, width), F32),
            pltpu.VMEM((rows * 56, width), F32),
            pltpu.VMEM((14 * SLOT, width), F32),
            pltpu.VMEM((2 * (terms + 1) * 56, width), F32),
            pltpu.VMEM((112, width), F32),
            pltpu.VMEM((terms, slots, slots), BF16),
            pltpu.VMEM((terms, slots, slots), BF16),
            pltpu.VMEM((slots, padded), BF16),
            pltpu.VMEM((slots, padded), BF16),
            pltpu.VMEM((slots, padded), BF16),
            pltpu.VMEM((terms, slots, 2 * width), BF16),
            pltpu.VMEM((terms, slots, 2 * width), BF16),
            pltpu.VMEM((terms, SLOT, width), F32),
            pltpu.VMEM((24, width), F32),
            pltpu.VMEM((8, width), F32),
            pltpu.VMEM((8, width), F32),
            pltpu.VMEM((chaos_n, 8, width), F32),
            pltpu.VMEM((space_n, 8, width), F32),
            pltpu.SemaphoreType.DMA((4,)),
            pltpu.SemaphoreType.DMA((30,)),
            pltpu.SemaphoreType.DMA((4, chaos_n)),
            pltpu.SemaphoreType.DMA((4, chaos_n)),
            pltpu.SemaphoreType.DMA((2, chaos_n)),
            pltpu.SemaphoreType.DMA((chaos_n,)),
            pltpu.SemaphoreType.DMA((space_n,)),
        ],
        compiler_params=pltpu.CompilerParams(
            collective_id=0, has_side_effects=True, vmem_limit_bytes=60 * 1024 * 1024
        ),
    )(
        start,
        source_term.reshape(own_modes, rows, width),
        conductivity.reshape(terms + 1, rows, width),
        lists,
    )
    split = 4 if rows % 32 == 0 else 1
    plain = pl.BlockSpec((own_modes, rows // split, width), lambda n: (0, n, 0))
    turned = pl.BlockSpec((flat // split, width), lambda n: (n, 0))
    outs = pl.pallas_call(
        functools.partial(combine, own_modes),
        grid=(split,),
        out_shape=(shape,) * 3,
        in_specs=[plain] + [turned] * 4 + [pl.BlockSpec((16, width), lambda n: (0, 0))],
        out_specs=(plain,) * 3,
    )(start, search, residual, image, precond, scale)
    return tuple(out.reshape(source_term.shape) for out in outs)


def solution(mesh):
    chaos_n, space_n = (mesh.shape["chaos"], mesh.shape["space"])
    field = P("chaos", "space", None, None)
    return jax.shard_map(
        functools.partial(per_device, chaos_n, space_n),
        mesh=mesh,
        in_specs=(field, field, P(None, "space", None, None), P(), P()),
        out_specs=(field, field, field),
        check_vma=False,
    )
```

```python
import functools

import jax
import jax.numpy as jnp
from jax import lax
from jax.experimental import pallas as pl
from jax.experimental.pallas import tpu as pltpu
from jax.sharding import PartitionSpec as P

CENTER_BOUND = 1.05
HALF_WIDTH = 0.95
FIRST_COEF = 4.0 * CENTER_BOUND / (2.0 * CENTER_BOUND * CENTER_BOUND - HALF_WIDTH * HALF_WIDTH)
SECOND_COEF = 2.0 / (2.0 * CENTER_BOUND * CENTER_BOUND - HALF_WIDTH * HALF_WIDTH)
SLOT = 16
F32 = jnp.float32
BF16 = jnp.bfloat16
MESH = pl.DeviceIdType.MESH


def al(value, unit):
    return pl.multiple_of(value, unit)


def kernel(
    chaos_n, space_n, terms, own_modes, rows,
    v_ref, f_ref, cond_ref, lists_ref,
    ss, mq, rr_ref, qq_ref, scale_ref,
    xv, xf, rr, qq, zr, zrm, zrp, zq, zqm, zqp,
    tv, tf, tr, tz, ts, tw, y0, y1,
    vxm, vxp, zxm, zxp, sxm, sxp, wxm, wxp,
    vym, vyp, zym, zyp, sym, syp, wym, wyp,
    cy, cxm, cxp, c0m, c0p, oc, ob, kf, kb, tb,
    gh, gl, oa, wh, wl, ph, plo, acc,
    sums, dots, dsum, dga, dgb,
    coef_sem, send_sem, a2a_sem, halo_sem, slab_sem, dota_sem, dotb_sem,
):
    me = lax.axis_index("chaos")
    sp = lax.axis_index("space")
    up = lax.rem(sp + 1, space_n)
    down = lax.rem(sp + space_n - 1, space_n)
    right = lax.rem(me + 1, chaos_n)
    left = lax.rem(me + chaos_n - 1, chaos_n)
    slots = chaos_n * SLOT
    flat = rows * SLOT
    width = v_ref.shape[-1]
    tiles = rows // 8
    per = -(-chaos_n // terms)
    lag = max(2, chaos_n // 2)

    def swing(i):
        return (2 * lax.rem(i, 2) - 1) * ((i + 1) // 2)

    def target(i):
        return lax.rem(me + chaos_n + swing(i), chaos_n)

    def source(i):
        return lax.rem(me + chaos_n - swing(i), chaos_n)

    def block(c):
        return pl.ds(al(c * 32, 32), 32)

    def low(c):
        return pl.ds(al(c * 32, 32), SLOT)

    def high(c):
        return pl.ds(al(c * 32 + SLOT, SLOT), SLOT)

    def half(c):
        return pl.ds(al(c * SLOT, SLOT), SLOT)

    def remote(src, dst, ssem, rsem, device):
        return pltpu.make_async_remote_copy(
            src_ref=src, dst_ref=dst, send_sem=ssem, recv_sem=rsem,
            device_id=device, device_id_type=MESH,
        )

    def drain(ref, count, sem):
        pltpu.make_async_copy(ref.at[pl.ds(0, count)], ref.at[pl.ds(0, count)], sem).wait()

    barrier = pltpu.get_barrier_semaphore()

    def greet_chaos(k, carry):
        pl.semaphore_signal(
            barrier, inc=1, device_id={"chaos": lax.rem(me + k, chaos_n)}, device_id_type=MESH
        )
        return carry

    lax.fori_loop(1, chaos_n, greet_chaos, 0)

    def greet_space(k, carry):
        pl.semaphore_signal(
            barrier, inc=1, device_id={"space": lax.rem(sp + k, space_n)}, device_id_type=MESH
        )
        return carry

    lax.fori_loop(1, space_n, greet_space, 0)

    blank = jnp.zeros((8, width), F32)

    def turn_in(from_ref, to_ref):
        def body(m, carry):
            for tile in range(tiles):
                to_ref[pl.ds(tile * 128 + m, 8, stride=SLOT), :] = from_ref[m, pl.ds(tile * 8, 8), :]
            return carry

        lax.fori_loop(0, own_modes, body, 0)
        for m in range(own_modes, SLOT):
            for tile in range(tiles):
                to_ref[pl.ds(tile * 128 + m, 8, stride=SLOT), :] = blank

    turn_in(v_ref, xv)
    for j in range(SLOT):
        for tile in range(tiles):
            value = cond_ref[j, pl.ds(tile * 8, 8), :] if j <= terms else blank
            cy[pl.ds(tile * 128 + j, 8, stride=SLOT), :] = value

    pl.semaphore_wait(barrier, chaos_n - 1 + space_n - 1)

    coef_copies = (
        remote(cy.at[block(me)], cxm.at[pl.ds(0, 32)], send_sem.at[0], coef_sem.at[0], {"space": up}),
        remote(cy.at[block(me)], cxp.at[pl.ds(0, 32)], send_sem.at[1], coef_sem.at[1], {"space": down}),
        remote(cond_ref.at[0], c0m, send_sem.at[2], coef_sem.at[2], {"space": up}),
        remote(cond_ref.at[0], c0p, send_sem.at[3], coef_sem.at[3], {"space": down}),
    )
    for copy in coef_copies:
        copy.start()

    def scatter(src, dst, which):
        def body(i, carry):
            c = target(i)
            remote(
                src.at[block(c)], dst.at[block(me)], send_sem.at[4 + which], a2a_sem.at[which].at[me], {"chaos": c}
            ).start()
            return carry

        lax.fori_loop(1, chaos_n, body, 0)
        dst[block(me), :] = src[block(me), :]

    def arrived(dst, which, i):
        @pl.when(i > 0)
        def _():
            c = source(i)
            remote(
                dst.at[block(c)], dst.at[block(c)], send_sem.at[4], a2a_sem.at[which].at[c], {"chaos": left}
            ).wait_recv()

    def spread_halo(src, halo, which, i):
        c = source(i)
        xm, xp, ym, yp = halo
        rsem = halo_sem.at[which].at[c]
        base = 8 + which * 4
        remote(src.at[block(c)], xm.at[block(c)], send_sem.at[base], rsem, {"space": up}).start()
        remote(src.at[block(c)], xp.at[block(c)], send_sem.at[base + 1], rsem, {"space": down}).start()
        remote(src.at[high(c)], ym.at[half(c)], send_sem.at[base + 2], rsem, {"chaos": right}).start()
        remote(src.at[low(c)], yp.at[half(c)], send_sem.at[base + 3], rsem, {"chaos": left}).start()

    def halo_arrived(which, i):
        c = source(i)
        pltpu.make_async_copy(xv.at[pl.ds(0, 96)], xv.at[pl.ds(0, 96)], halo_sem.at[which].at[c]).wait()

    def around(src, halo, c, r, h):
        xm, xp, ym, yp = halo
        at = pl.ds(al(c * 32 + r * SLOT + h * 8, 8), 8)
        other = pl.ds(al(c * 32 + (1 - r) * SLOT + h * 8, 8), 8)
        side = pl.ds(al(c * SLOT + h * 8, 8), 8)
        v = src[at, :]
        return (
            v,
            xm[at, :],
            xp[at, :],
            ym[side, :] if r == 0 else src[other, :],
            src[other, :] if r == 0 else yp[side, :],
            pltpu.roll(v, 1, 1),
            pltpu.roll(v, width - 1, 1),
        )

    scatter(xv, tv, 0)
    turn_in(f_ref, xf)
    tf[block(me), :] = xf[block(me), :]

    def send_source(i):
        @pl.when(i > 0)
        def _():
            c = target(i)
            remote(
                xf.at[block(c)], tf.at[block(me)], send_sem.at[5], a2a_sem.at[1].at[me], {"chaos": c}
            ).start()


    lane = lax.broadcasted_iota(jnp.int32, (1, width), 1)
    zm_mask = jnp.where(lane > 0, 0.5, 0.0).astype(F32)
    zp_mask = jnp.where(lane < width - 1, 0.5, 0.0).astype(F32)
    xm_mask = jnp.where(sp > 0, 0.5, 0.0).astype(F32)
    xp_mask = jnp.where(sp < space_n - 1, 0.5, 0.0).astype(F32)

    for copy in coef_copies:
        copy.wait()

    for r in range(2):
        y = me * 2 + r
        cn = cy[pl.ds(al(y * SLOT, SLOT), SLOT), :]
        cm = cy[pl.ds(al(lax.rem(y + rows - 1, rows) * SLOT, SLOT), SLOT), :]
        cp = cy[pl.ds(al(lax.rem(y + 1, rows) * SLOT, SLOT), SLOT), :]
        ym_mask = jnp.where(y > 0, 0.5, 0.0).astype(F32)
        yp_mask = jnp.where(y < rows - 1, 0.5, 0.0).astype(F32)
        total = 3.0 * cn
        near = (
            (cxm[pl.ds(r * SLOT, SLOT), :], xm_mask),
            (cxp[pl.ds(r * SLOT, SLOT), :], xp_mask),
            (cm, ym_mask),
            (cp, yp_mask),
            (pltpu.roll(cn, 1, 1), zm_mask),
            (pltpu.roll(cn, width - 1, 1), zp_mask),
        )
        for n, (other, mask) in enumerate(near):
            total = total + other * mask
            kf[pl.ds((r * 7 + n + 1) * SLOT, SLOT), :] = (cn + other) * mask
        kf[pl.ds(r * 7 * SLOT, SLOT), :] = total
    for r in range(2):
        for j in range(terms + 1):
            for n in range(7):
                row = kf[pl.ds((r * 7 + n) * SLOT + j, 1), :]
                kb[pl.ds(((r * (terms + 1) + j) * 7 + n) * 8, 8), :] = jnp.broadcast_to(row, (8, width))
        inv = 1.0 / kf[pl.ds(r * 7 * SLOT, 1), :]
        tb[pl.ds(r * 56 + 48, 8), :] = jnp.broadcast_to(inv, (8, width))
        for n in range(6):
            row = SECOND_COEF * kf[pl.ds((r * 7 + n + 1) * SLOT, 1), :] * inv
            tb[pl.ds(r * 56 + n * 8, 8), :] = jnp.broadcast_to(row, (8, width))

    c0 = cond_ref[0]
    yrow = lax.broadcasted_iota(jnp.int32, (rows, 1), 0)
    near = (
        (c0m[...], xm_mask),
        (c0p[...], xp_mask),
        (pltpu.roll(c0, 1, 0), jnp.where(yrow > 0, 0.5, 0.0).astype(F32)),
        (pltpu.roll(c0, rows - 1, 0), jnp.where(yrow < rows - 1, 0.5, 0.0).astype(F32)),
        (pltpu.roll(c0, 1, 1), zm_mask),
        (pltpu.roll(c0, width - 1, 1), zp_mask),
    )
    diagonal = 3.0 * c0
    for other, mask in near:
        diagonal = diagonal + other * mask
    inverse = 1.0 / diagonal
    oc[6] = inverse
    for n, (other, mask) in enumerate(near):
        oc[n] = SECOND_COEF * ((c0 + other) * mask) * inverse

    def spread(tile, carry):
        for n in range(7):
            group = oc[n, pl.ds(al(tile * 8, 8), 8), :]
            for i in range(8):
                at = al((tile * 56 + i * 7 + n) * 8, 8)
                ob[pl.ds(at, 8), :] = jnp.broadcast_to(group[i : i + 1, :], (8, width))
        return carry

    lax.fori_loop(0, tiles, spread, 0)

    def products(src, halo, which, y, i):
        halo_arrived(which, i)
        c = source(i)
        to = half(c)
        for r in range(2):
            for h in range(2):
                near = around(src, halo, c, r, h)
                for j in range(terms + 1):
                    base = (r * (terms + 1) + j) * 56
                    value = kb[pl.ds(base, 8), :] * near[0]
                    for n in range(1, 7):
                        value = value - kb[pl.ds(base + n * 8, 8), :] * near[n]
                    if j == 0:
                        y[pl.ds(al(c * 32 + r * SLOT + h * 8, 8), 8), :] = value
                    else:
                        acc[j - 1, pl.ds(h * 8, 8), :] = value
            for j in range(terms):
                value = acc[j, pl.ds(0, SLOT), :]
                top = value.astype(BF16)
                ph[j, to, pl.ds(r * width, width)] = top
                plo[j, to, pl.ds(r * width, width)] = (value - top.astype(F32)).astype(BF16)

    def mix(y):
        def body(j, total):
            a, b = (gh[j], ph[j])
            total = total + jnp.dot(a, b, preferred_element_type=F32)
            total = total + jnp.dot(a, plo[j], preferred_element_type=F32)
            return total + jnp.dot(gl[j], b, preferred_element_type=F32)

        total = lax.fori_loop(0, terms, body, jnp.zeros((slots, 2 * width), F32))
        for c in range(chaos_n):
            for r in range(2):
                at = pl.ds(c * 32 + r * SLOT, SLOT)
                y[at, :] = y[at, :] + total[c * SLOT : (c + 1) * SLOT, r * width : (r + 1) * width]

    index = lax.broadcasted_iota(jnp.int32, (slots, lists_ref.shape[-1]), 0).astype(F32)
    nt = (((1,), (1,)), ((), ()))

    def build(j, carry):
        first = lists_ref[pl.ds(j, 1), :]
        second = lists_ref[pl.ds(j + terms, 1), :]
        first = first + (SLOT - own_modes) * jnp.floor((first + 0.5) * (1.0 / own_modes))
        second = second + (SLOT - own_modes) * jnp.floor((second + 0.5) * (1.0 / own_modes))
        weight = lists_ref[pl.ds(j + 2 * terms, 1), :]
        weight_high = weight.astype(BF16).astype(F32)
        weight_low = weight - weight_high
        oa[...] = jnp.where(index == first, 1.0, 0.0).astype(BF16)
        here = index == second
        wh[...] = jnp.where(here, weight_high, 0.0).astype(BF16)
        wl[...] = jnp.where(here, weight_low, 0.0).astype(BF16)
        a, b, c = (oa[...], wh[...], wl[...])
        g = lax.dot_general(a, b, nt, preferred_element_type=F32)
        g = g + lax.dot_general(a, c, nt, preferred_element_type=F32)
        g = g + lax.dot_general(b, a, nt, preferred_element_type=F32)
        g = g + lax.dot_general(c, a, nt, preferred_element_type=F32)
        top = g.astype(BF16)
        gh[j] = top
        gl[j] = (g - top.astype(F32)).astype(BF16)

        def step(n, inner):
            i = j * per + n

            @pl.when(i < chaos_n)
            def _():
                arrived(tv, 0, i)
                spread_halo(tv, (vxm, vxp, vym, vyp), 0, i)
                send_source(i)

            @pl.when((i >= lag) & (i < chaos_n))
            def _():
                products(tv, (vxm, vxp, vym, vyp), 0, y0, i - lag)

            return inner

        return lax.fori_loop(0, per, step, carry)

    lax.fori_loop(0, terms, build, 0)

    def rest(i, carry):
        products(tv, (vxm, vxp, vym, vyp), 0, y0, i)
        return carry

    lax.fori_loop(chaos_n - lag, chaos_n, rest, 0)
    mix(y0)

    sums[...] = jnp.zeros_like(sums)

    def weigh(row, value):
        sums[pl.ds(row * 8, 8), :] = sums[pl.ds(row * 8, 8), :] + value

    def residual_step(i):
        arrived(tf, 1, i)
        c = source(i)
        for r in range(2):
            inv = tb[pl.ds(r * 56 + 48, 8), :]
            for h in range(2):
                at = pl.ds(al(c * 32 + r * SLOT + h * 8, 8), 8)
                value = tf[at, :] - y0[at, :]
                tr[at, :] = value
                tz[at, :] = value * inv
        spread_halo(tz, (zxm, zxp, zym, zyp), 1, i)

    def search_step(i):
        halo_arrived(1, i)
        c = source(i)
        for r in range(2):
            coef = [tb[pl.ds(r * 56 + n * 8, 8), :] for n in range(6)]
            for h in range(2):
                at = pl.ds(al(c * 32 + r * SLOT + h * 8, 8), 8)
                near = around(tz, (zxm, zxp, zym, zyp), c, r, h)
                value = (FIRST_COEF - SECOND_COEF) * near[0]
                for n in range(6):
                    value = value + coef[n] * near[n + 1]
                ts[at, :] = value
                weigh(0, value * tr[at, :])
        spread_halo(ts, (sxm, sxp, sym, syp), 2, i)

    def each(step):
        def body(i, carry):
            step(i)
            return carry

        lax.fori_loop(0, chaos_n, body, 0)

    each(residual_step)
    each(search_step)

    def last_step(i):
        c = source(i)

        @pl.when(i > 0)
        def _():
            remote(
                tr.at[block(c)], rr.at[block(me)], send_sem.at[6], a2a_sem.at[2].at[me], {"chaos": c}
            ).start()

        products(ts, (sxm, sxp, sym, syp), 2, y1, i)

    each(last_step)
    rr[block(me), :] = tr[block(me), :]
    heights = slots // (4 * SLOT)

    def pick(ref, j, part):
        return jnp.concatenate(
            [ref[j, pl.ds((z * 4 + part * 2) * SLOT, 2 * SLOT), :] for z in range(heights)], axis=0
        )

    for part in range(2):

        def body(j, total):
            a, b = (pick(gh, j, part), ph[j])
            total = total + jnp.dot(a, b, preferred_element_type=F32)
            total = total + jnp.dot(a, plo[j], preferred_element_type=F32)
            return total + jnp.dot(pick(gl, j, part), b, preferred_element_type=F32)

        total = lax.fori_loop(0, terms, body, jnp.zeros((slots // 2, 2 * width), F32))
        for n in range(2 * heights):
            c = n // 2 * 4 + part * 2 + n % 2
            for r in range(2):
                at = pl.ds(c * 32 + r * SLOT, SLOT)
                y1[at, :] = y1[at, :] + total[n * SLOT : (n + 1) * SLOT, r * width : (r + 1) * width]

        def send_image(n, carry):
            c = target(chaos_n - n)

            @pl.when(lax.rem(c, 4) // 2 == part)
            def _():
                remote(
                    y1.at[block(c)], qq.at[block(me)], send_sem.at[7], a2a_sem.at[3].at[me], {"chaos": c}
                ).start()

            return carry

        lax.fori_loop(1, chaos_n, send_image, 0)
    qq[block(me), :] = y1[block(me), :]

    def image_step(i, carry):
        c = source(i)
        for r in range(2):
            inv = tb[pl.ds(r * 56 + 48, 8), :]
            for h in range(2):
                at = pl.ds(al(c * 32 + r * SLOT + h * 8, 8), 8)
                tw[at, :] = y1[at, :] * inv
        spread_halo(tw, (wxm, wxp, wym, wyp), 3, i)
        return carry

    lax.fori_loop(0, chaos_n, image_step, 0)

    def slab_step(src, which, z, zm, zp, base, number, i):
        arrived(src, which, i)
        c = source(i)
        for r in range(2):
            inv = ob[pl.ds(al((c * 2 + r) * 56 + 48, 8), 8), :]
            for h in range(2):
                at = pl.ds(al(c * 32 + r * SLOT + h * 8, 8), 8)
                z[at, :] = src[at, :] * inv
        rsem = slab_sem.at[number].at[c]
        remote(z.at[block(c)], zm.at[block(c)], send_sem.at[base], rsem, {"space": up}).start()
        remote(z.at[block(c)], zp.at[block(c)], send_sem.at[base + 1], rsem, {"space": down}).start()

    def slab_finish(z, zm, zp, number, to, field, keep, i):
        c = source(i)
        pltpu.make_async_copy(xv.at[pl.ds(0, 64)], xv.at[pl.ds(0, 64)], slab_sem.at[number].at[c]).wait()
        for r in range(2):
            line = c * 2 + r
            prev = lax.rem(line + rows - 1, rows)
            after = lax.rem(line + 1, rows)
            coef = [ob[pl.ds(al(line * 56 + n * 8, 8), 8), :] for n in range(6)]
            for h in range(2):
                at = pl.ds(al(line * SLOT + h * 8, 8), 8)
                v = z[at, :]
                near = (
                    zm[at, :],
                    zp[at, :],
                    z[pl.ds(al(prev * SLOT + h * 8, 8), 8), :],
                    z[pl.ds(al(after * SLOT + h * 8, 8), 8), :],
                    pltpu.roll(v, 1, 1),
                    pltpu.roll(v, width - 1, 1),
                )
                value = (FIRST_COEF - SECOND_COEF) * v
                for n in range(6):
                    value = value + coef[n] * near[n]
                to[at, :] = value
                keep[at, :] = field[at, :]

    each(lambda i: slab_step(rr, 2, zr, zrm, zrp, 24, 0, i))

    def image_dot(i, carry):
        halo_arrived(3, i)
        c = source(i)
        for r in range(2):
            coef = [tb[pl.ds(r * 56 + n * 8, 8), :] for n in range(6)]
            for h in range(2):
                at = pl.ds(al(c * 32 + r * SLOT + h * 8, 8), 8)
                near = around(tw, (wxm, wxp, wym, wyp), c, r, h)
                value = (FIRST_COEF - SECOND_COEF) * near[0]
                for n in range(6):
                    value = value + coef[n] * near[n + 1]
                image = y1[at, :]
                weigh(1, image * ts[at, :])
                weigh(2, image * value)
        return carry

    lax.fori_loop(0, chaos_n, image_dot, 0)
    dots[...] = blank
    for n in range(3):
        dots[pl.ds(n, 1), :] = jnp.sum(sums[pl.ds(n * 8, 8), :], axis=0, keepdims=True)

    def tell(k, carry):
        c = lax.rem(me + k, chaos_n)
        remote(dots, dga.at[k], send_sem.at[28], dota_sem.at[k], {"chaos": c}).start()
        return carry

    lax.fori_loop(1, chaos_n, tell, 0)

    each(lambda i: slab_finish(zr, zrm, zrp, 0, ss, rr, rr_ref, i))

    slack = max(2, chaos_n // 4)
    turn = chaos_n - slack

    def tail(n, carry):
        @pl.when(n < chaos_n)
        def _():
            slab_step(qq, 3, zq, zqm, zqp, 26, 1, chaos_n - 1 - n)

        @pl.when(n >= slack)
        def _():
            slab_finish(zq, zqm, zqp, 1, mq, qq, qq_ref, chaos_n - 1 - n + slack)

        return carry

    lax.fori_loop(0, turn, tail, 0)

    def hear(k, total):
        remote(dots, dga.at[k], send_sem.at[28], dota_sem.at[k], {"chaos": left}).wait_recv()
        return total + dga[k]

    dsum[...] = lax.fori_loop(1, chaos_n, hear, dots[...])

    def tell_space(k, carry):
        there = lax.rem(sp + k, space_n)
        remote(dsum, dgb.at[k], send_sem.at[29], dotb_sem.at[k], {"space": there}).start()
        return carry

    lax.fori_loop(1, space_n, tell_space, 0)

    lax.fori_loop(turn, chaos_n + slack, tail, 0)

    def hear_space(k, total):
        remote(dsum, dgb.at[k], send_sem.at[29], dotb_sem.at[k], {"space": up}).wait_recv()
        return total + dgb[k]

    whole = lax.fori_loop(1, space_n, hear_space, dsum[...])
    lanes = jnp.sum(whole, axis=1, keepdims=True)
    energy_start, curvature, image_energy = (lanes[0:1, :], lanes[1:2, :], lanes[2:3, :])
    step_size = energy_start / curvature
    energy_next = energy_start - 2.0 * step_size * curvature + step_size * step_size * image_energy
    ratio = 1.0 + energy_next / energy_start
    scale_ref[pl.ds(0, 8), :] = jnp.broadcast_to(step_size, (8, width))
    scale_ref[pl.ds(8, 8), :] = jnp.broadcast_to(ratio, (8, width))

    for n, ref in enumerate((xv, xf, tr, y1)):
        drain(ref, (chaos_n - 1) * 32, send_sem.at[4 + n])
    for n, ref in enumerate((tv, tz, ts, tw)):
        for m, count in enumerate((flat, flat, flat // 2, flat // 2)):
            drain(ref, count, send_sem.at[8 + n * 4 + m])
    for n, ref in enumerate((zr, zq)):
        for m in range(2):
            drain(ref, flat, send_sem.at[24 + n * 2 + m])
    pltpu.make_async_copy(dga.at[pl.ds(1, chaos_n - 1)], dga.at[pl.ds(1, chaos_n - 1)], send_sem.at[28]).wait()
    pltpu.make_async_copy(dgb.at[pl.ds(1, space_n - 1)], dgb.at[pl.ds(1, space_n - 1)], send_sem.at[29]).wait()


def combine(own_modes, v_ref, ss, rr, qq, mq, scale_ref, sol_ref, res_ref, dir_ref):
    step_all = scale_ref[pl.ds(0, 8), :]
    ratio_all = scale_ref[pl.ds(8, 8), :]
    tiles = v_ref.shape[1] // 8

    def turn_out(m, carry):
        for tile in range(tiles):
            where = pl.ds(tile * 128 + m, 8, stride=SLOT)
            there = pl.ds(tile * 8, 8)
            search = ss[where, :]
            sol_ref[m, there, :] = v_ref[m, there, :] + step_all * search
            res_ref[m, there, :] = rr[where, :] - step_all * qq[where, :]
            dir_ref[m, there, :] = ratio_all * search - step_all * mq[where, :]
        return carry

    lax.fori_loop(0, own_modes, turn_out, 0)


def per_device(chaos_n, space_n, source_term, start_field, conductivity, pair_modes, pair_weight):
    own_modes, _, rows, width = source_term.shape
    terms, pairs = pair_weight.shape
    slots = chaos_n * SLOT
    flat = rows * SLOT
    padded = -(-pairs // 128) * 128
    lists = jnp.concatenate(
        [pair_modes[:, :, 0].astype(F32), pair_modes[:, :, 1].astype(F32), pair_weight], axis=0
    )
    lists = jnp.pad(lists, ((0, 0), (0, padded - pairs)), constant_values=-1.0)
    field = pltpu.VMEM((flat, width), F32)
    half = pltpu.VMEM((flat // 2, width), F32)
    vmem = pl.BlockSpec(memory_space=pltpu.VMEM)
    shape = jax.ShapeDtypeStruct((own_modes, rows, width), F32)
    flat_shape = jax.ShapeDtypeStruct((flat, width), F32)
    start = start_field.reshape(own_modes, rows, width)
    search, precond, residual, image, scale = pl.pallas_call(
        functools.partial(kernel, chaos_n, space_n, terms, own_modes, rows),
        out_shape=(flat_shape,) * 4 + (jax.ShapeDtypeStruct((16, width), F32),),
        in_specs=[vmem] * 4,
        out_specs=(vmem,) * 5,
        scratch_shapes=[field] * 26
        + [half] * 8
        + [field]
        + [pltpu.VMEM((32, width), F32)] * 2
        + [pltpu.VMEM((rows, width), F32)] * 2
        + [
            pltpu.VMEM((7, rows, width), F32),
            pltpu.VMEM((rows * 56, width), F32),
            pltpu.VMEM((14 * SLOT, width), F32),
            pltpu.VMEM((2 * (terms + 1) * 56, width), F32),
            pltpu.VMEM((112, width), F32),
            pltpu.VMEM((terms, slots, slots), BF16),
            pltpu.VMEM((terms, slots, slots), BF16),
            pltpu.VMEM((slots, padded), BF16),
            pltpu.VMEM((slots, padded), BF16),
            pltpu.VMEM((slots, padded), BF16),
            pltpu.VMEM((terms, slots, 2 * width), BF16),
            pltpu.VMEM((terms, slots, 2 * width), BF16),
            pltpu.VMEM((terms, SLOT, width), F32),
            pltpu.VMEM((24, width), F32),
            pltpu.VMEM((8, width), F32),
            pltpu.VMEM((8, width), F32),
            pltpu.VMEM((chaos_n, 8, width), F32),
            pltpu.VMEM((space_n, 8, width), F32),
            pltpu.SemaphoreType.DMA((4,)),
            pltpu.SemaphoreType.DMA((30,)),
            pltpu.SemaphoreType.DMA((4, chaos_n)),
            pltpu.SemaphoreType.DMA((4, chaos_n)),
            pltpu.SemaphoreType.DMA((2, chaos_n)),
            pltpu.SemaphoreType.DMA((chaos_n,)),
            pltpu.SemaphoreType.DMA((space_n,)),
        ],
        compiler_params=pltpu.CompilerParams(
            collective_id=0, has_side_effects=True, vmem_limit_bytes=60 * 1024 * 1024
        ),
    )(
        start,
        source_term.reshape(own_modes, rows, width),
        conductivity.reshape(terms + 1, rows, width),
        lists,
    )
    split = 4 if rows % 32 == 0 else 1
    plain = pl.BlockSpec((own_modes, rows // split, width), lambda n: (0, n, 0))
    turned = pl.BlockSpec((flat // split, width), lambda n: (n, 0))
    outs = pl.pallas_call(
        functools.partial(combine, own_modes),
        grid=(split,),
        out_shape=(shape,) * 3,
        in_specs=[plain] + [turned] * 4 + [pl.BlockSpec((16, width), lambda n: (0, 0))],
        out_specs=(plain,) * 3,
    )(start, search, residual, image, precond, scale)
    return tuple(out.reshape(source_term.shape) for out in outs)


def solution(mesh):
    chaos_n, space_n = (mesh.shape["chaos"], mesh.shape["space"])
    field = P("chaos", "space", None, None)
    return jax.shard_map(
        functools.partial(per_device, chaos_n, space_n),
        mesh=mesh,
        in_specs=(field, field, P(None, "space", None, None), P(), P()),
        out_specs=(field, field, field),
        check_vma=False,
    )
```

```python
import functools

import jax
import jax.numpy as jnp
from jax import lax
from jax.experimental import pallas as pl
from jax.experimental.pallas import tpu as pltpu
from jax.sharding import PartitionSpec as P

CENTER_BOUND = 1.05
HALF_WIDTH = 0.95
FIRST_COEF = 4.0 * CENTER_BOUND / (2.0 * CENTER_BOUND * CENTER_BOUND - HALF_WIDTH * HALF_WIDTH)
SECOND_COEF = 2.0 / (2.0 * CENTER_BOUND * CENTER_BOUND - HALF_WIDTH * HALF_WIDTH)
SLOT = 16
F32 = jnp.float32
BF16 = jnp.bfloat16
MESH = pl.DeviceIdType.MESH


def al(value, unit):
    return pl.multiple_of(value, unit)


def kernel(
    chaos_n, space_n, terms, own_modes, rows,
    v_ref, f_ref, cond_ref, modes_ref, weight_ref,
    ss, mq, rr_ref, qq_ref, scale_ref,
    xv, xf, rr, qq, zr, zrm, zrp, zq, zqm, zqp,
    tv, tf, tr, tz, ts, tw, y0, y1,
    vxm, vxp, zxm, zxp, sxm, sxp, wxm, wxp,
    vym, vyp, zym, zyp, sym, syp, wym, wyp,
    cy, cxm, cxp, c0m, c0p, oc, ob, kf, kb, tb,
    gh, gl, oa, wh, wl, ph, plo, acc,
    lists_ref, sums, dots, dsum, dga, dgb,
    coef_sem, send_sem, a2a_sem, halo_sem, slab_sem, dota_sem, dotb_sem,
):
    me = lax.axis_index("chaos")
    sp = lax.axis_index("space")
    up = lax.rem(sp + 1, space_n)
    down = lax.rem(sp + space_n - 1, space_n)
    right = lax.rem(me + 1, chaos_n)
    left = lax.rem(me + chaos_n - 1, chaos_n)
    slots = chaos_n * SLOT
    flat = rows * SLOT
    width = v_ref.shape[-1]
    tiles = rows // 8
    per = -(-chaos_n // terms)
    lag = chaos_n

    def swing(i):
        return (2 * lax.rem(i, 2) - 1) * ((i + 1) // 2)

    def target(i):
        return lax.rem(me + chaos_n + swing(i), chaos_n)

    def source(i):
        return lax.rem(me + chaos_n - swing(i), chaos_n)

    def block(c):
        return pl.ds(al(c * 32, 32), 32)

    def low(c):
        return pl.ds(al(c * 32, 32), SLOT)

    def high(c):
        return pl.ds(al(c * 32 + SLOT, SLOT), SLOT)

    def half(c):
        return pl.ds(al(c * SLOT, SLOT), SLOT)

    def remote(src, dst, ssem, rsem, device):
        return pltpu.make_async_remote_copy(
            src_ref=src, dst_ref=dst, send_sem=ssem, recv_sem=rsem,
            device_id=device, device_id_type=MESH,
        )

    def drain(ref, count, sem):
        pltpu.make_async_copy(ref.at[pl.ds(0, count)], ref.at[pl.ds(0, count)], sem).wait()

    barrier = pltpu.get_barrier_semaphore()

    def greet_chaos(k, carry):
        pl.semaphore_signal(
            barrier, inc=1, device_id={"chaos": lax.rem(me + k, chaos_n)}, device_id_type=MESH
        )
        return carry

    lax.fori_loop(1, chaos_n, greet_chaos, 0)

    def greet_space(k, carry):
        pl.semaphore_signal(
            barrier, inc=1, device_id={"space": lax.rem(sp + k, space_n)}, device_id_type=MESH
        )
        return carry

    lax.fori_loop(1, space_n, greet_space, 0)

    blank = jnp.zeros((8, width), F32)

    def turn_in(from_ref, to_ref):
        def body(m, carry):
            for tile in range(tiles):
                to_ref[pl.ds(tile * 128 + m, 8, stride=SLOT), :] = from_ref[m, pl.ds(tile * 8, 8), :]
            return carry

        lax.fori_loop(0, own_modes, body, 0)
        for m in range(own_modes, SLOT):
            for tile in range(tiles):
                to_ref[pl.ds(tile * 128 + m, 8, stride=SLOT), :] = blank

    turn_in(v_ref, xv)
    for j in range(SLOT):
        for tile in range(tiles):
            value = cond_ref[j, pl.ds(tile * 8, 8), :] if j <= terms else blank
            cy[pl.ds(tile * 128 + j, 8, stride=SLOT), :] = value

    pl.semaphore_wait(barrier, chaos_n - 1 + space_n - 1)

    coef_copies = (
        remote(cy.at[block(me)], cxm.at[pl.ds(0, 32)], send_sem.at[0], coef_sem.at[0], {"space": up}),
        remote(cy.at[block(me)], cxp.at[pl.ds(0, 32)], send_sem.at[1], coef_sem.at[1], {"space": down}),
        remote(cond_ref.at[0], c0m, send_sem.at[2], coef_sem.at[2], {"space": up}),
        remote(cond_ref.at[0], c0p, send_sem.at[3], coef_sem.at[3], {"space": down}),
    )
    for copy in coef_copies:
        copy.start()

    def scatter(src, dst, which):
        def body(i, carry):
            c = target(i)
            remote(
                src.at[block(c)], dst.at[block(me)], send_sem.at[4 + which], a2a_sem.at[which].at[me], {"chaos": c}
            ).start()
            return carry

        lax.fori_loop(1, chaos_n, body, 0)
        dst[block(me), :] = src[block(me), :]

    def arrived(dst, which, i):
        @pl.when(i > 0)
        def _():
            c = source(i)
            remote(
                dst.at[block(c)], dst.at[block(c)], send_sem.at[4], a2a_sem.at[which].at[c], {"chaos": left}
            ).wait_recv()

    def spread_halo(src, halo, which, i):
        c = source(i)
        xm, xp, ym, yp = halo
        rsem = halo_sem.at[which].at[c]
        base = 8 + which * 4
        remote(src.at[block(c)], xm.at[block(c)], send_sem.at[base], rsem, {"space": up}).start()
        remote(src.at[block(c)], xp.at[block(c)], send_sem.at[base + 1], rsem, {"space": down}).start()
        remote(src.at[high(c)], ym.at[half(c)], send_sem.at[base + 2], rsem, {"chaos": right}).start()
        remote(src.at[low(c)], yp.at[half(c)], send_sem.at[base + 3], rsem, {"chaos": left}).start()

    def halo_arrived(which, i):
        c = source(i)
        pltpu.make_async_copy(xv.at[pl.ds(0, 96)], xv.at[pl.ds(0, 96)], halo_sem.at[which].at[c]).wait()

    def around(src, halo, c, r, h):
        xm, xp, ym, yp = halo
        at = pl.ds(al(c * 32 + r * SLOT + h * 8, 8), 8)
        other = pl.ds(al(c * 32 + (1 - r) * SLOT + h * 8, 8), 8)
        side = pl.ds(al(c * SLOT + h * 8, 8), 8)
        v = src[at, :]
        return (
            v,
            xm[at, :],
            xp[at, :],
            ym[side, :] if r == 0 else src[other, :],
            src[other, :] if r == 0 else yp[side, :],
            pltpu.roll(v, 1, 1),
            pltpu.roll(v, width - 1, 1),
        )

    scatter(xv, tv, 0)
    turn_in(f_ref, xf)
    tf[block(me), :] = xf[block(me), :]

    def send_source(i):
        @pl.when(i > 0)
        def _():
            c = target(i)
            remote(
                xf.at[block(c)], tf.at[block(me)], send_sem.at[5], a2a_sem.at[1].at[me], {"chaos": c}
            ).start()


    lane = lax.broadcasted_iota(jnp.int32, (1, width), 1)
    zm_mask = jnp.where(lane > 0, 0.5, 0.0).astype(F32)
    zp_mask = jnp.where(lane < width - 1, 0.5, 0.0).astype(F32)
    xm_mask = jnp.where(sp > 0, 0.5, 0.0).astype(F32)
    xp_mask = jnp.where(sp < space_n - 1, 0.5, 0.0).astype(F32)

    for copy in coef_copies:
        copy.wait()

    for r in range(2):
        y = me * 2 + r
        cn = cy[pl.ds(al(y * SLOT, SLOT), SLOT), :]
        cm = cy[pl.ds(al(lax.rem(y + rows - 1, rows) * SLOT, SLOT), SLOT), :]
        cp = cy[pl.ds(al(lax.rem(y + 1, rows) * SLOT, SLOT), SLOT), :]
        ym_mask = jnp.where(y > 0, 0.5, 0.0).astype(F32)
        yp_mask = jnp.where(y < rows - 1, 0.5, 0.0).astype(F32)
        total = 3.0 * cn
        near = (
            (cxm[pl.ds(r * SLOT, SLOT), :], xm_mask),
            (cxp[pl.ds(r * SLOT, SLOT), :], xp_mask),
            (cm, ym_mask),
            (cp, yp_mask),
            (pltpu.roll(cn, 1, 1), zm_mask),
            (pltpu.roll(cn, width - 1, 1), zp_mask),
        )
        for n, (other, mask) in enumerate(near):
            total = total + other * mask
            kf[pl.ds((r * 7 + n + 1) * SLOT, SLOT), :] = (cn + other) * mask
        kf[pl.ds(r * 7 * SLOT, SLOT), :] = total
    for r in range(2):
        for j in range(terms + 1):
            for n in range(7):
                row = kf[pl.ds((r * 7 + n) * SLOT + j, 1), :]
                kb[pl.ds(((r * (terms + 1) + j) * 7 + n) * 8, 8), :] = jnp.broadcast_to(row, (8, width))
        inv = 1.0 / kf[pl.ds(r * 7 * SLOT, 1), :]
        tb[pl.ds(r * 56 + 48, 8), :] = jnp.broadcast_to(inv, (8, width))
        for n in range(6):
            row = SECOND_COEF * kf[pl.ds((r * 7 + n + 1) * SLOT, 1), :] * inv
            tb[pl.ds(r * 56 + n * 8, 8), :] = jnp.broadcast_to(row, (8, width))

    c0 = cond_ref[0]
    yrow = lax.broadcasted_iota(jnp.int32, (rows, 1), 0)
    near = (
        (c0m[...], xm_mask),
        (c0p[...], xp_mask),
        (pltpu.roll(c0, 1, 0), jnp.where(yrow > 0, 0.5, 0.0).astype(F32)),
        (pltpu.roll(c0, rows - 1, 0), jnp.where(yrow < rows - 1, 0.5, 0.0).astype(F32)),
        (pltpu.roll(c0, 1, 1), zm_mask),
        (pltpu.roll(c0, width - 1, 1), zp_mask),
    )
    diagonal = 3.0 * c0
    for other, mask in near:
        diagonal = diagonal + other * mask
    inverse = 1.0 / diagonal
    oc[6] = inverse
    for n, (other, mask) in enumerate(near):
        oc[n] = SECOND_COEF * ((c0 + other) * mask) * inverse

    def spread(tile, carry):
        for n in range(7):
            group = oc[n, pl.ds(al(tile * 8, 8), 8), :]
            for i in range(8):
                at = al((tile * 56 + i * 7 + n) * 8, 8)
                ob[pl.ds(at, 8), :] = jnp.broadcast_to(group[i : i + 1, :], (8, width))
        return carry

    lax.fori_loop(0, tiles, spread, 0)

    def products(src, halo, which, y, i):
        halo_arrived(which, i)
        c = source(i)
        to = half(c)
        for r in range(2):
            for h in range(2):
                near = around(src, halo, c, r, h)
                for j in range(terms + 1):
                    base = (r * (terms + 1) + j) * 56
                    value = kb[pl.ds(base, 8), :] * near[0]
                    for n in range(1, 7):
                        value = value - kb[pl.ds(base + n * 8, 8), :] * near[n]
                    if j == 0:
                        y[pl.ds(al(c * 32 + r * SLOT + h * 8, 8), 8), :] = value
                    else:
                        acc[j - 1, pl.ds(h * 8, 8), :] = value
            for j in range(terms):
                value = acc[j, pl.ds(0, SLOT), :]
                top = value.astype(BF16)
                ph[j, to, pl.ds(r * width, width)] = top
                plo[j, to, pl.ds(r * width, width)] = (value - top.astype(F32)).astype(BF16)

    def mix(y):
        def body(j, total):
            a, b = (gh[j], ph[j])
            total = total + jnp.dot(a, b, preferred_element_type=F32)
            total = total + jnp.dot(a, plo[j], preferred_element_type=F32)
            return total + jnp.dot(gl[j], b, preferred_element_type=F32)

        total = lax.fori_loop(0, terms, body, jnp.zeros((slots, 2 * width), F32))
        for c in range(chaos_n):
            for r in range(2):
                at = pl.ds(c * 32 + r * SLOT, SLOT)
                y[at, :] = y[at, :] + total[c * SLOT : (c + 1) * SLOT, r * width : (r + 1) * width]

    pairs = weight_ref.shape[-1]
    lists_ref[...] = jnp.full_like(lists_ref, -1.0)
    for n in range(2):
        lists_ref[pl.ds(n * terms, terms), pl.ds(0, pairs)] = modes_ref[n].astype(F32)
    lists_ref[pl.ds(2 * terms, terms), pl.ds(0, pairs)] = weight_ref[...]

    index = lax.broadcasted_iota(jnp.int32, (slots, lists_ref.shape[-1]), 0).astype(F32)
    nt = (((1,), (1,)), ((), ()))

    def build(j, carry):
        first = lists_ref[pl.ds(j, 1), :]
        second = lists_ref[pl.ds(j + terms, 1), :]
        first = first + (SLOT - own_modes) * jnp.floor((first + 0.5) * (1.0 / own_modes))
        second = second + (SLOT - own_modes) * jnp.floor((second + 0.5) * (1.0 / own_modes))
        weight = lists_ref[pl.ds(j + 2 * terms, 1), :]
        weight_high = weight.astype(BF16).astype(F32)
        weight_low = weight - weight_high
        oa[...] = jnp.where(index == first, 1.0, 0.0).astype(BF16)
        here = index == second
        wh[...] = jnp.where(here, weight_high, 0.0).astype(BF16)
        wl[...] = jnp.where(here, weight_low, 0.0).astype(BF16)
        a, b, c = (oa[...], wh[...], wl[...])
        g = lax.dot_general(a, b, nt, preferred_element_type=F32)
        g = g + lax.dot_general(a, c, nt, preferred_element_type=F32)
        g = g + lax.dot_general(b, a, nt, preferred_element_type=F32)
        g = g + lax.dot_general(c, a, nt, preferred_element_type=F32)
        top = g.astype(BF16)
        gh[j] = top
        gl[j] = (g - top.astype(F32)).astype(BF16)

        def step(n, inner):
            i = j * per + n

            @pl.when(i < chaos_n)
            def _():
                arrived(tv, 0, i)
                spread_halo(tv, (vxm, vxp, vym, vyp), 0, i)
                send_source(i)

            @pl.when((i >= lag) & (i < chaos_n))
            def _():
                products(tv, (vxm, vxp, vym, vyp), 0, y0, i - lag)

            return inner

        return lax.fori_loop(0, per, step, carry)

    lax.fori_loop(0, terms, build, 0)

    def rest(i, carry):
        products(tv, (vxm, vxp, vym, vyp), 0, y0, i)
        return carry

    lax.fori_loop(chaos_n - lag, chaos_n, rest, 0)
    mix(y0)

    sums[...] = jnp.zeros_like(sums)

    def weigh(row, value):
        sums[pl.ds(row * 8, 8), :] = sums[pl.ds(row * 8, 8), :] + value

    def residual_step(i):
        arrived(tf, 1, i)
        c = source(i)
        for r in range(2):
            inv = tb[pl.ds(r * 56 + 48, 8), :]
            for h in range(2):
                at = pl.ds(al(c * 32 + r * SLOT + h * 8, 8), 8)
                value = tf[at, :] - y0[at, :]
                tr[at, :] = value
                tz[at, :] = value * inv
        spread_halo(tz, (zxm, zxp, zym, zyp), 1, i)

    def search_step(i):
        halo_arrived(1, i)
        c = source(i)
        for r in range(2):
            coef = [tb[pl.ds(r * 56 + n * 8, 8), :] for n in range(6)]
            for h in range(2):
                at = pl.ds(al(c * 32 + r * SLOT + h * 8, 8), 8)
                near = around(tz, (zxm, zxp, zym, zyp), c, r, h)
                value = (FIRST_COEF - SECOND_COEF) * near[0]
                for n in range(6):
                    value = value + coef[n] * near[n + 1]
                ts[at, :] = value
                weigh(0, value * tr[at, :])
        spread_halo(ts, (sxm, sxp, sym, syp), 2, i)

    def each(step):
        def body(i, carry):
            step(i)
            return carry

        lax.fori_loop(0, chaos_n, body, 0)

    each(residual_step)
    each(search_step)

    def last_step(i):
        c = source(i)

        @pl.when(i > 0)
        def _():
            remote(
                tr.at[block(c)], rr.at[block(me)], send_sem.at[6], a2a_sem.at[2].at[me], {"chaos": c}
            ).start()

        products(ts, (sxm, sxp, sym, syp), 2, y1, i)

    each(last_step)
    rr[block(me), :] = tr[block(me), :]
    mix(y1)
    scatter(y1, qq, 3)

    def image_step(i, carry):
        c = source(i)
        for r in range(2):
            inv = tb[pl.ds(r * 56 + 48, 8), :]
            for h in range(2):
                at = pl.ds(al(c * 32 + r * SLOT + h * 8, 8), 8)
                tw[at, :] = y1[at, :] * inv
        spread_halo(tw, (wxm, wxp, wym, wyp), 3, i)
        return carry

    lax.fori_loop(0, chaos_n, image_step, 0)

    def slab_step(src, which, z, zm, zp, base, number):
        def body(i, carry):
            arrived(src, which, i)
            c = source(i)
            for r in range(2):
                inv = ob[pl.ds(al((c * 2 + r) * 56 + 48, 8), 8), :]
                for h in range(2):
                    at = pl.ds(al(c * 32 + r * SLOT + h * 8, 8), 8)
                    z[at, :] = src[at, :] * inv
            rsem = slab_sem.at[number].at[c]
            remote(z.at[block(c)], zm.at[block(c)], send_sem.at[base], rsem, {"space": up}).start()
            remote(z.at[block(c)], zp.at[block(c)], send_sem.at[base + 1], rsem, {"space": down}).start()
            return carry

        lax.fori_loop(0, chaos_n, body, 0)

    def slab_finish(z, zm, zp, number, to, field, keep):
        def body(i, carry):
            c = source(i)
            pltpu.make_async_copy(xv.at[pl.ds(0, 64)], xv.at[pl.ds(0, 64)], slab_sem.at[number].at[c]).wait()
            for r in range(2):
                line = c * 2 + r
                prev = lax.rem(line + rows - 1, rows)
                after = lax.rem(line + 1, rows)
                coef = [ob[pl.ds(al(line * 56 + n * 8, 8), 8), :] for n in range(6)]
                for h in range(2):
                    at = pl.ds(al(line * SLOT + h * 8, 8), 8)
                    v = z[at, :]
                    near = (
                        zm[at, :],
                        zp[at, :],
                        z[pl.ds(al(prev * SLOT + h * 8, 8), 8), :],
                        z[pl.ds(al(after * SLOT + h * 8, 8), 8), :],
                        pltpu.roll(v, 1, 1),
                        pltpu.roll(v, width - 1, 1),
                    )
                    value = (FIRST_COEF - SECOND_COEF) * v
                    for n in range(6):
                        value = value + coef[n] * near[n]
                    to[at, :] = value
                    keep[at, :] = field[at, :]
            return carry

        lax.fori_loop(0, chaos_n, body, 0)

    slab_step(rr, 2, zr, zrm, zrp, 24, 0)

    def image_dot(i, carry):
        halo_arrived(3, i)
        c = source(i)
        for r in range(2):
            coef = [tb[pl.ds(r * 56 + n * 8, 8), :] for n in range(6)]
            for h in range(2):
                at = pl.ds(al(c * 32 + r * SLOT + h * 8, 8), 8)
                near = around(tw, (wxm, wxp, wym, wyp), c, r, h)
                value = (FIRST_COEF - SECOND_COEF) * near[0]
                for n in range(6):
                    value = value + coef[n] * near[n + 1]
                image = y1[at, :]
                weigh(1, image * ts[at, :])
                weigh(2, image * value)
        return carry

    lax.fori_loop(0, chaos_n, image_dot, 0)
    dots[...] = blank
    for n in range(3):
        dots[pl.ds(n, 1), :] = jnp.sum(sums[pl.ds(n * 8, 8), :], axis=0, keepdims=True)

    def tell(k, carry):
        c = lax.rem(me + k, chaos_n)
        remote(dots, dga.at[k], send_sem.at[28], dota_sem.at[k], {"chaos": c}).start()
        return carry

    lax.fori_loop(1, chaos_n, tell, 0)

    slab_finish(zr, zrm, zrp, 0, ss, rr, rr_ref)

    slab_step(qq, 3, zq, zqm, zqp, 26, 1)

    def hear(k, total):
        remote(dots, dga.at[k], send_sem.at[28], dota_sem.at[k], {"chaos": left}).wait_recv()
        return total + dga[k]

    dsum[...] = lax.fori_loop(1, chaos_n, hear, dots[...])

    def tell_space(k, carry):
        there = lax.rem(sp + k, space_n)
        remote(dsum, dgb.at[k], send_sem.at[29], dotb_sem.at[k], {"space": there}).start()
        return carry

    lax.fori_loop(1, space_n, tell_space, 0)

    slab_finish(zq, zqm, zqp, 1, mq, qq, qq_ref)

    def hear_space(k, total):
        remote(dsum, dgb.at[k], send_sem.at[29], dotb_sem.at[k], {"space": up}).wait_recv()
        return total + dgb[k]

    whole = lax.fori_loop(1, space_n, hear_space, dsum[...])
    lanes = jnp.sum(whole, axis=1, keepdims=True)
    energy_start, curvature, image_energy = (lanes[0:1, :], lanes[1:2, :], lanes[2:3, :])
    step_size = energy_start / curvature
    energy_next = energy_start - 2.0 * step_size * curvature + step_size * step_size * image_energy
    ratio = 1.0 + energy_next / energy_start
    scale_ref[pl.ds(0, 8), :] = jnp.broadcast_to(step_size, (8, width))
    scale_ref[pl.ds(8, 8), :] = jnp.broadcast_to(ratio, (8, width))

    for n, ref in enumerate((xv, xf, tr, y1)):
        drain(ref, (chaos_n - 1) * 32, send_sem.at[4 + n])
    for n, ref in enumerate((tv, tz, ts, tw)):
        for m, count in enumerate((flat, flat, flat // 2, flat // 2)):
            drain(ref, count, send_sem.at[8 + n * 4 + m])
    for n, ref in enumerate((zr, zq)):
        for m in range(2):
            drain(ref, flat, send_sem.at[24 + n * 2 + m])
    pltpu.make_async_copy(dga.at[pl.ds(1, chaos_n - 1)], dga.at[pl.ds(1, chaos_n - 1)], send_sem.at[28]).wait()
    pltpu.make_async_copy(dgb.at[pl.ds(1, space_n - 1)], dgb.at[pl.ds(1, space_n - 1)], send_sem.at[29]).wait()


def combine(own_modes, v_ref, ss, rr, qq, mq, scale_ref, sol_ref, res_ref, dir_ref):
    step_all = scale_ref[pl.ds(0, 8), :]
    ratio_all = scale_ref[pl.ds(8, 8), :]
    tiles = v_ref.shape[1] // 8

    def turn_out(m, carry):
        for tile in range(tiles):
            where = pl.ds(tile * 128 + m, 8, stride=SLOT)
            there = pl.ds(tile * 8, 8)
            search = ss[where, :]
            sol_ref[m, there, :] = v_ref[m, there, :] + step_all * search
            res_ref[m, there, :] = rr[where, :] - step_all * qq[where, :]
            dir_ref[m, there, :] = ratio_all * search - step_all * mq[where, :]
        return carry

    lax.fori_loop(0, own_modes, turn_out, 0)


def per_device(chaos_n, space_n, source_term, start_field, conductivity, pair_modes, pair_weight):
    own_modes, _, rows, width = source_term.shape
    terms, pairs = pair_weight.shape
    slots = chaos_n * SLOT
    flat = rows * SLOT
    padded = -(-pairs // 128) * 128
    field = pltpu.VMEM((flat, width), F32)
    half = pltpu.VMEM((flat // 2, width), F32)
    vmem = pl.BlockSpec(memory_space=pltpu.VMEM)
    shape = jax.ShapeDtypeStruct((own_modes, rows, width), F32)
    flat_shape = jax.ShapeDtypeStruct((flat, width), F32)
    start = start_field.reshape(own_modes, rows, width)
    search, precond, residual, image, scale = pl.pallas_call(
        functools.partial(kernel, chaos_n, space_n, terms, own_modes, rows),
        out_shape=(flat_shape,) * 4 + (jax.ShapeDtypeStruct((16, width), F32),),
        in_specs=[vmem] * 5,
        out_specs=(vmem,) * 5,
        scratch_shapes=[field] * 26
        + [half] * 8
        + [field]
        + [pltpu.VMEM((32, width), F32)] * 2
        + [pltpu.VMEM((rows, width), F32)] * 2
        + [
            pltpu.VMEM((7, rows, width), F32),
            pltpu.VMEM((rows * 56, width), F32),
            pltpu.VMEM((14 * SLOT, width), F32),
            pltpu.VMEM((2 * (terms + 1) * 56, width), F32),
            pltpu.VMEM((112, width), F32),
            pltpu.VMEM((terms, slots, slots), BF16),
            pltpu.VMEM((terms, slots, slots), BF16),
            pltpu.VMEM((slots, padded), BF16),
            pltpu.VMEM((slots, padded), BF16),
            pltpu.VMEM((slots, padded), BF16),
            pltpu.VMEM((terms, slots, 2 * width), BF16),
            pltpu.VMEM((terms, slots, 2 * width), BF16),
            pltpu.VMEM((terms, SLOT, width), F32),
            pltpu.VMEM((3 * terms, padded), F32),
            pltpu.VMEM((24, width), F32),
            pltpu.VMEM((8, width), F32),
            pltpu.VMEM((8, width), F32),
            pltpu.VMEM((chaos_n, 8, width), F32),
            pltpu.VMEM((space_n, 8, width), F32),
            pltpu.SemaphoreType.DMA((4,)),
            pltpu.SemaphoreType.DMA((30,)),
            pltpu.SemaphoreType.DMA((4, chaos_n)),
            pltpu.SemaphoreType.DMA((4, chaos_n)),
            pltpu.SemaphoreType.DMA((2, chaos_n)),
            pltpu.SemaphoreType.DMA((chaos_n,)),
            pltpu.SemaphoreType.DMA((space_n,)),
        ],
        compiler_params=pltpu.CompilerParams(
            collective_id=0, has_side_effects=True, vmem_limit_bytes=60 * 1024 * 1024
        ),
    )(
        start,
        source_term.reshape(own_modes, rows, width),
        conductivity.reshape(terms + 1, rows, width),
        jnp.transpose(pair_modes, (2, 0, 1)),
        pair_weight,
    )
    split = 2 if rows % 16 == 0 else 1
    plain = pl.BlockSpec((own_modes, rows // split, width), lambda n: (0, n, 0))
    turned = pl.BlockSpec((flat // split, width), lambda n: (n, 0))
    outs = pl.pallas_call(
        functools.partial(combine, own_modes),
        grid=(split,),
        out_shape=(shape,) * 3,
        in_specs=[plain] + [turned] * 4 + [pl.BlockSpec((16, width), lambda n: (0, 0))],
        out_specs=(plain,) * 3,
    )(start, search, residual, image, precond, scale)
    return tuple(out.reshape(source_term.shape) for out in outs)


def solution(mesh):
    chaos_n, space_n = (mesh.shape["chaos"], mesh.shape["space"])
    field = P("chaos", "space", None, None)
    return jax.shard_map(
        functools.partial(per_device, chaos_n, space_n),
        mesh=mesh,
        in_specs=(field, field, P(None, "space", None, None), P(), P()),
        out_specs=(field, field, field),
        check_vma=False,
    )
```
